32 devices in a mesh: lat: 8 (over z, core), lon: 4 (over y, x).
Axes of the slice: x: 2, y: 2, z: 4, core: 2. Of those that a mesh axis runs over, the one named last changes fastest.
Arguments:
- pedersen: float32 [16, 1024, 2048], P(None, 'lat', 'lon'), may hold values from 0.2 to 2
- hall_conductivity: float32 [16, 1024, 2048], P(None, 'lat', 'lon'), may hold values from 0.1 to 1.5
- east_wind: float32 [16, 1024, 2048], P(None, 'lat', 'lon'), may hold values from -6 to 6
- north_wind: float32 [16, 1024, 2048], P(None, 'lat', 'lon'), may hold values from -6 to 6
- ion_density: float32 [3, 1024, 2048], P(None, 'lat', 'lon'), may hold values from 0.5 to 2
Outputs:
- potential: float32 [1024, 2048], P('lat', 'lon')
- ion_update: float32 [3, 1024, 2048], P(None, 'lat', 'lon')
The draws below stay inside these ranges and needn't reach their ends.
All inputs are finite; a program needn't handle non-finite values. Where the reference program divides by a largest or mean magnitude, that divisor is 1e-20 or more.
Results may differ from the reference program's by a relative error of at most 0.00002.
Values sent between devices are 32-bit elements; how exact they have to be, the bound alone decides.
A program may use at most 192 MiB of HBM per device.

```python
import math
import jax
import jax.numpy as jnp
from jax import lax

LEV = 16
SWEEPS = 16
NLAT = 1024
NLON = 2048


def steps_of(own_key, extent, pieces, least, top_value):
    level, own = 1.0, jax.random.fold_in(own_key, 6)
    for axis_at, shards_of in pieces:
        heights = jnp.exp(jax.random.uniform(jax.random.fold_in(own, axis_at), (shards_of,), jnp.float32, least / len(pieces), top_value / len(pieces)))
        level = level * jnp.repeat(heights, extent[axis_at] // shards_of).reshape([-1 if axis == axis_at else 1 for axis in range(len(extent))])
    return level


def bell_draw(rng, extent, scale, bound, split=(), kind=jnp.bfloat16):
    entries = scale * jax.random.normal(rng, extent, jnp.float32)
    if split:
        entries = entries * steps_of(rng, extent, split, -0.22, 0.18)
    return jnp.clip(entries, -bound, bound).astype(kind)


def setup_inputs(seed: int = 0) -> dict:
    key_list = jax.random.split(jax.random.key(seed), 6)
    return {
        "pedersen": jnp.clip(jnp.exp(math.log(2.0) - 2.3025851 * jax.random.uniform(key_list[0], (LEV, NLAT, NLON), jnp.float32) ** steps_of(key_list[0], (LEV, NLAT, NLON), ((1, 8), (2, 4)), -0.2, 0.2)), 0.2, 2.0),
        "hall_conductivity": jnp.clip(jnp.exp(math.log(1.5) - 2.7080502 * jax.random.uniform(key_list[1], (LEV, NLAT, NLON), jnp.float32) ** steps_of(key_list[1], (LEV, NLAT, NLON), ((1, 8), (2, 4)), -0.2, 0.2)), 0.1, 1.5),
        "east_wind": bell_draw(key_list[2], (LEV, NLAT, NLON), 1.0, 6.0, ((1, 8), (2, 4)), jnp.float32),
        "north_wind": bell_draw(key_list[3], (LEV, NLAT, NLON), 1.0, 6.0, ((1, 8), (2, 4)), jnp.float32),
        "ion_density": jnp.clip(jnp.exp(math.log(2.0) - 1.3862944 * jax.random.uniform(key_list[4], (3, NLAT, NLON), jnp.float32) ** steps_of(key_list[4], (3, NLAT, NLON), ((1, 8), (2, 4)), -0.2, 0.2)), 0.5, 2.0),
    }


DAMPING = 0.0001
LOW_BOUND = 0.05
HIGH_BOUND = 2.0
COURANT = 0.8
MOBILITY = (1.0, 0.6, 0.3)
NEIGHBOURS = ((-1, 0, 1.0), (1, 0, 1.0), (0, -1, 1.0), (0, 1, 1.0), (-1, -1, 0.5), (-1, 1, 0.5), (1, -1, 0.5), (1, 1, 0.5))


def thickness():
    levels = jnp.arange(LEV, dtype=jnp.float32)
    return (0.5 + levels / LEV) / LEV


def chebyshev_factors():
    theta = 0.5 * (HIGH_BOUND + LOW_BOUND)
    delta = 0.5 * (HIGH_BOUND - LOW_BOUND)
    sigma_one = theta / delta
    rho_prev = 1.0 / sigma_one
    first_list = []
    second_list = []
    for sweep in range(SWEEPS):
        rho_next = 1.0 / (2.0 * sigma_one - rho_prev)
        first_list.append(rho_next * rho_prev)
        second_list.append(2.0 * rho_next / delta)
        rho_prev = rho_next
    return theta, first_list, second_list


def extend(field, width):
    padded = jnp.pad(field, ((width, width), (0, 0)))
    return jnp.concatenate([padded[:, -width:], padded, padded[:, :width]], axis=1)


def window(array, shift_lat, shift_lon):
    height = array.shape[0] - 2
    breadth = array.shape[1] - 2
    return array[1 + shift_lat:1 + shift_lat + height, 1 + shift_lon:1 + shift_lon + breadth]


def stencil(sigma_ext):
    center = window(sigma_ext, 0, 0)
    weights = []
    diagonal = jnp.zeros_like(center) + DAMPING
    for shift_lat, shift_lon, factor in NEIGHBOURS:
        weight = factor * 0.5 * (center + window(sigma_ext, shift_lat, shift_lon))
        weights.append(weight)
    for weight in weights:
        diagonal = diagonal + weight
    return weights, diagonal


def apply_operator(field_ext, weights, diagonal):
    result = diagonal * window(field_ext, 0, 0)
    for index_pair, (shift_lat, shift_lon, factor) in enumerate(NEIGHBOURS):
        result = result - weights[index_pair] * window(field_ext, shift_lat, shift_lon)
    return result


def divergence(east_ext, north_ext):
    return 0.5 * (window(east_ext, 0, 1) - window(east_ext, 0, -1)) + 0.5 * (window(north_ext, 1, 0) - window(north_ext, -1, 0))


def advect(density_ext, cross_east, cross_north):
    density = window(density_ext, 0, 0)
    result = density - jnp.maximum(cross_east, 0.0) * (density - window(density_ext, 0, -1))
    result = result - jnp.minimum(cross_east, 0.0) * (window(density_ext, 0, 1) - density)
    result = result - jnp.maximum(cross_north, 0.0) * (density - window(density_ext, -1, 0))
    result = result - jnp.minimum(cross_north, 0.0) * (window(density_ext, 1, 0) - density)
    return result


def reference(pedersen, hall_conductivity, east_wind, north_wind, ion_density):
    layer = thickness()

    def accumulate(level, totals):
        sigma_p = pedersen[level]
        sigma_h = hall_conductivity[level]
        wind_e = east_wind[level]
        wind_n = north_wind[level]
        return (totals[0] + layer[level] * sigma_p,
                totals[1] + layer[level] * (sigma_p * wind_e + sigma_h * wind_n),
                totals[2] + layer[level] * (sigma_p * wind_n - sigma_h * wind_e))

    zeros = jnp.zeros(pedersen.shape[1:], jnp.float32)
    sigma, current_east, current_north = lax.fori_loop(0, LEV, accumulate, (zeros, zeros, zeros))
    sigma = sigma + sigma[::-1]
    current_east = current_east + current_east[::-1]
    current_north = current_north + current_north[::-1]
    weights, diagonal = stencil(extend(sigma, 1))
    source = divergence(extend(current_east, 1), extend(current_north, 1))
    theta, first_list, second_list = chebyshev_factors()
    solution = jnp.zeros_like(source)
    update = source / diagonal / theta
    for sweep in range(SWEEPS):
        solution = solution + update
        image = apply_operator(extend(solution, 1), weights, diagonal)
        scaled = (source - image) / diagonal
        update = first_list[sweep] * update + second_list[sweep] * scaled
    potential = solution
    potential_ext = extend(potential, 1)
    drift_east = -0.5 * (window(potential_ext, 1, 0) - window(potential_ext, -1, 0))
    drift_north = 0.5 * (window(potential_ext, 0, 1) - window(potential_ext, 0, -1))
    fastest = jnp.max(jnp.abs(drift_east) + jnp.abs(drift_north))
    time_step = COURANT / (fastest + 1e-6)
    results = []
    for species in range(3):
        cross_east = MOBILITY[species] * time_step * drift_east
        cross_north = MOBILITY[species] * time_step * drift_north
        results.append(advect(extend(ion_density[species], 1), cross_east, cross_north))
    return potential, jnp.stack(results)
```

```python
import functools

import jax
import jax.numpy as jnp
from jax import lax
from jax.experimental import pallas as pl
from jax.experimental.pallas import tpu as pltpu
from jax.sharding import PartitionSpec as P

SWEEPS = 16
DAMPING = 0.0001
LOW_BOUND = 0.05
HIGH_BOUND = 2.0
COURANT = 0.8
MOBILITY = (1.0, 0.6, 0.3)
MESH = pl.DeviceIdType.MESH
HALO = 24
F32 = jnp.float32


def chebyshev_factors():
    theta = 0.5 * (HIGH_BOUND + LOW_BOUND)
    delta = 0.5 * (HIGH_BOUND - LOW_BOUND)
    sigma_one = theta / delta
    rho_prev = 1.0 / sigma_one
    first_list = []
    second_list = []
    for sweep in range(SWEEPS):
        rho_next = 1.0 / (2.0 * sigma_one - rho_prev)
        first_list.append(rho_next * rho_prev)
        second_list.append(2.0 * rho_next / delta)
        rho_prev = rho_next
    return (theta, first_list, second_list)


def kernel(
    nlat, nlon, lev, rows, lt,
    coef, ped_h, hall_h, east_h, north_h, ion_h,
    pot_h, upd_h,
    ped, hall, east, north,
    ion, ion_fr, ion_fl,
    sig, cur_e, cur_n, e_fr, e_fl, s_one, t_out, sig_rx, t_rx,
    S, src, pk_l, pk_r, rx_fr, rx_fl,
    g, r, sp, x, d, u, w,
    flux, upd, mx, rx_lat, mx2, rx_lon,
    sem_in, sem_ion, sem_out, ss, rs, ss_lat, rs_lat, ss_lon, rs_lon,
):
    n_rt = rows // 8
    nt = lt + 1
    me_lat = lax.axis_index("lat")
    me_lon = lax.axis_index("lon")
    has_up = me_lat > 0
    has_dn = me_lat < nlat - 1
    up = (jnp.maximum(me_lat - 1, 0), me_lon)
    dn = (jnp.minimum(me_lat + 1, nlat - 1), me_lon)
    lf = (me_lat, lax.rem(me_lon + nlon - 1, nlon))
    rt = (me_lat, lax.rem(me_lon + 1, nlon))
    mirror = (nlat - 1 - me_lat, me_lon)

    order = [0, n_rt - 1] + list(range(1, n_rt - 1))
    hbm_in = (ped_h, hall_h, east_h, north_h)
    vm_in = (ped, hall, east, north)

    def in_copy(a, row, slot):
        return pltpu.make_async_copy(
            hbm_in[a].at[:, pl.ds(row, 8), :], vm_in[a].at[:, pl.ds(row, 8), :], sem_in.at[slot, a]
        )

    def ion_copy(s, t):
        return pltpu.make_async_copy(
            ion_h.at[s, :, t * 128 : (t + 1) * 128], ion.at[s, t, 8 : 8 + rows], sem_ion.at[s, t]
        )

    for c in order[:2]:
        for a in range(4):
            in_copy(a, 8 * c, c).start()
    for s in range(3):
        for t in range(lt):
            ion_copy(s, t).start()
    for c in order[2:]:
        for a in range(4):
            in_copy(a, 8 * c, c).start()

    barrier = pltpu.get_barrier_semaphore()
    for o in range(1, nlat):
        pl.semaphore_signal(
            barrier, inc=1, device_id=(lax.rem(me_lat + o, nlat), me_lon), device_id_type=MESH
        )
    for o in range(1, nlon):
        pl.semaphore_signal(
            barrier, inc=1, device_id=(me_lat, lax.rem(me_lon + o, nlon)), device_id_type=MESH
        )
    pl.semaphore_wait(barrier, nlat + nlon - 2)

    def rcopy(src_ref, dst_ref, k, dev):
        return pltpu.make_async_remote_copy(
            src_ref=src_ref, dst_ref=dst_ref, send_sem=ss.at[k], recv_sem=rs.at[k],
            device_id=dev, device_id_type=MESH,
        )

    lane = lax.broadcasted_iota(jnp.int32, (8, 128), 1)
    sub = lax.broadcasted_iota(jnp.int32, (8, 128), 0)

    def shifts(v):
        m = len(v)
        a = [pltpu.roll(t, 1, 1) for t in v]
        b = [pltpu.roll(t, 127, 1) for t in v]
        left = [jnp.where(lane == 0, a[j - 1], a[j]) for j in range(m)]
        right = [jnp.where(lane == 127, b[(j + 1) % m], b[j]) for j in range(m)]
        return left, right

    def smooth(v):
        left, right = shifts(v)
        return [t + 0.5 * (p + q) for t, p, q in zip(v, left, right)]

    def rev8(v):
        v = pltpu.roll(v, 4, 0)
        for b in (2, 1):
            v = jnp.where((sub & b) == 0, pltpu.roll(v, 8 - b, 0), pltpu.roll(v, b, 0))
        return v

    weight = [(0.5 + l / lev) / lev for l in range(lev)]

    def columns(c):
        row = pl.multiple_of(8 * c, 8)
        for a in range(4):
            in_copy(a, row, c).wait()
        for t in range(lt):
            at = (pl.ds(row, 8), slice(t * 128, (t + 1) * 128))
            acc = [jnp.zeros((8, 128), F32)] * 3
            for l in range(lev):
                p, h = weight[l] * ped[(l,) + at], weight[l] * hall[(l,) + at]
                e, n = east[(l,) + at], north[(l,) + at]
                acc = [acc[0] + p, acc[1] + (p * e + h * n), acc[2] + (p * n - h * e)]
            sig[t, pl.ds(row, 8), :] = acc[0]
            cur_e[t, pl.ds(row, 8), :] = acc[1]
            cur_n[t, pl.ds(row + 8, 8), :] = acc[2]

    def both(lo, hi):
        @pl.loop(lo, hi)
        def _(c):
            columns(c)

    both(0, 1)
    both(n_rt - 1, n_rt)
    n_up = rcopy(cur_n.at[:, 8:16], cur_n.at[:, rows + 8 : rows + 16], 0, up)
    n_dn = rcopy(cur_n.at[:, rows : rows + 8], cur_n.at[:, 0:8], 1, dn)
    i_up = rcopy(ion.at[:, :, 8:16], ion.at[:, :, rows + 8 : rows + 16], 2, up)
    i_dn = rcopy(ion.at[:, :, rows : rows + 8], ion.at[:, :, 0:8], 3, dn)
    i_lf = rcopy(ion.at[:, 0, 8 : 8 + rows], ion_fr, 4, lf)
    i_rt = rcopy(ion.at[:, lt - 1, 8 : 8 + rows], ion_fl, 5, rt)

    for s in range(3):
        for t in range(lt):
            ion_copy(s, t).wait()

    @pl.when(has_up)
    def _():
        n_up.start()
        i_up.start()

    @pl.when(has_dn)
    def _():
        n_dn.start()
        i_dn.start()

    @pl.when(jnp.logical_not(has_up))
    def _():
        cur_n[:, 0:8, :] = jnp.zeros((lt, 8, 128), F32)
        ion[:, :, 0:8, :] = jnp.zeros((3, lt, 8, 128), F32)

    @pl.when(jnp.logical_not(has_dn))
    def _():
        cur_n[:, rows + 8 : rows + 16, :] = jnp.zeros((lt, 8, 128), F32)
        ion[:, :, rows + 8 : rows + 16, :] = jnp.zeros((3, lt, 8, 128), F32)

    pieces = 4
    per = n_rt // pieces
    sig_copies = []
    for q in range(pieces):
        both(max(1, q * per), min(n_rt - 1, (q + 1) * per))
        band = slice(q * per * 8, (q + 1) * per * 8)
        copy = rcopy(sig.at[:, band], sig_rx.at[:, band], 6 + q, mirror)
        copy.start()
        sig_copies.append(copy)

    e_lf = rcopy(cur_e.at[0], e_fr, 10, lf)
    e_rt = rcopy(cur_e.at[lt - 1], e_fl, 11, rt)
    e_lf.start()
    e_rt.start()
    i_lf.start()
    i_rt.start()

    @pl.when(has_dn)
    def _():
        n_up.wait_recv()

    @pl.when(has_up)
    def _():
        n_dn.wait_recv()

    e_lf.wait_recv()
    e_rt.wait_recv()

    t_copies = []
    for q in range(pieces):
        @pl.loop(q * per, (q + 1) * per)
        def _(c):
            row = pl.multiple_of(8 * c, 8)
            tiles = [cur_e[t, pl.ds(row, 8), :] for t in range(lt)]
            tiles.append(jnp.where(lane < 64, e_fr[pl.ds(row, 8), :], e_fl[pl.ds(row, 8), :]))
            left, right = shifts(tiles)
            for t in range(lt):
                d_lon = 0.5 * (right[t] - left[t])
                d_lat = 0.5 * (cur_n[t, pl.ds(row + 9, 8), :] - cur_n[t, pl.ds(row + 7, 8), :])
                s_one[t, pl.ds(row, 8), :] = d_lon + d_lat
                t_out[t, pl.ds(row, 8), :] = d_lon - d_lat

        band = slice(q * per * 8, (q + 1) * per * 8)
        copy = rcopy(t_out.at[:, band], t_rx.at[:, band], 12 + q, mirror)
        copy.start()
        t_copies.append(copy)

    def zero_rows(ref, lo, hi):
        ref[0:lt, lo:hi, :] = jnp.zeros((lt, hi - lo, 128), F32)

    @pl.when(jnp.logical_not(has_up))
    def _():
        zero_rows(S, 0, HALO)
        zero_rows(src, 0, HALO)

    @pl.when(jnp.logical_not(has_dn))
    def _():
        zero_rows(S, HALO + rows, 2 * HALO + rows)
        zero_rows(src, HALO + rows, 2 * HALO + rows)

    def combine(own, rx, out, q):
        @pl.loop((pieces - 1 - q) * per, (pieces - q) * per)
        def _(c):
            row = pl.multiple_of(8 * c, 8)
            back = pl.multiple_of(rows - 8 - 8 * c, 8)
            for t in range(lt):
                out[t, pl.ds(row + HALO, 8), :] = own[t, pl.ds(row, 8), :] + rev8(
                    rx[t, pl.ds(back, 8), :]
                )

    for q in range(pieces):
        sig_copies[q].wait_recv()
        combine(sig, sig_rx, S, q)
    for q in range(pieces):
        t_copies[q].wait_recv()
        combine(s_one, t_rx, src, q)

    lo_in, lo_out = slice(HALO, 2 * HALO), slice(0, HALO)
    hi_in, hi_out = slice(rows, rows + HALO), slice(rows + HALO, rows + 2 * HALO)
    mid = slice(HALO, HALO + rows)
    ups = [
        rcopy(f.at[0:lt, lo_in], f.at[0:lt, hi_out], 16 + k, up) for k, f in enumerate((S, src))
    ]
    dns = [
        rcopy(f.at[0:lt, hi_in], f.at[0:lt, lo_out], 18 + k, dn) for k, f in enumerate((S, src))
    ]

    @pl.when(has_up)
    def _():
        for c in ups:
            c.start()

    @pl.when(has_dn)
    def _():
        for c in dns:
            c.start()

    def pack(lo, hi):
        @pl.loop(lo // 8, hi // 8)
        def _(c):
            at = pl.ds(pl.multiple_of(8 * c, 8), 8)
            pk_l[at, :] = jnp.where(lane < 64, S[0, at, :], pltpu.roll(src[0, at, :], 64, 1))
            pk_r[at, :] = jnp.where(
                lane >= 64, S[lt - 1, at, :], pltpu.roll(src[lt - 1, at, :], 64, 1)
            )

    lons = []

    def send_lon(part, k):
        lons.append(rcopy(pk_l.at[part], rx_fr.at[part], k, lf))
        lons.append(rcopy(pk_r.at[part], rx_fl.at[part], k + 1, rt))
        lons[-2].start()
        lons[-1].start()

    pack(HALO, HALO + rows)
    send_lon(mid, 20)

    @pl.when(has_up)
    def _():
        for c in dns:
            c.wait_recv()

    pack(0, HALO)
    send_lon(lo_out, 22)

    @pl.when(has_dn)
    def _():
        for c in ups:
            c.wait_recv()

    pack(HALO + rows, 2 * HALO + rows)
    send_lon(hi_out, 24)
    for c in lons:
        c.wait_recv()

    n_ext = (rows + 2 * HALO) // 8
    total = rows * nlat

    @pl.loop(0, n_ext)
    def _(c):
        at = pl.ds(pl.multiple_of(8 * c, 8), 8)
        fr, fl = rx_fr[at, :], rx_fl[at, :]
        s_halo = jnp.where(lane < 64, fr, fl)
        S[lt, at, :] = s_halo
        src[lt, at, :] = pltpu.roll(jnp.where(lane >= 64, fr, fl), 64, 1)
        tiles = [S[t, at, :] for t in range(lt)] + [s_halo]
        for t, v in enumerate(smooth(tiles)):
            u[t, at, :] = v
            w[t, at, :] = jnp.zeros((8, 128), F32)

    theta = 0.5 * (HIGH_BOUND + LOW_BOUND)

    def column_conv(ref, t, row):
        return (
            ref[t, pl.ds(row - 1, 8), :] + ref[t, pl.ds(row + 1, 8), :]
        ) + 2.0 * ref[t, pl.ds(row, 8), :]

    @pl.loop(1, n_ext - 1)
    def _(c):
        row = pl.multiple_of(8 * c, 8)
        at = pl.ds(row, 8)
        where = sub + (row - HALO + me_lat * rows)
        inside = (where >= 0) & (where < total)
        for t in range(nt):
            s = S[t, at, :]
            diag = DAMPING + 0.5 * (4.0 * s + column_conv(u, t, row))
            inv = jnp.where(inside, 1.0 / diag, 0.0)
            half = 0.5 * inv
            r[t, at, :] = half
            g[t, at, :] = half * s
            first = src[t, at, :] * inv
            sp[t, at, :] = first
            d[t, at, :] = first * (1.0 / theta)
            x[t, at, :] = jnp.zeros((8, 128), F32)

    def sweep(k, lo, hi):
        c1 = coef[0, k]
        c2 = coef[1, k]

        @pl.loop(lo, hi, unroll=2)
        def _(c):
            at = pl.ds(pl.multiple_of(8 * c, 8), 8)
            xs = [x[t, at, :] + d[t, at, :] for t in range(nt)]
            ys = [S[t, at, :] * xs[t] for t in range(nt)]
            us = smooth(xs)
            ws = smooth(ys)
            for t in range(nt):
                x[t, at, :] = xs[t]
                u[t, at, :] = us[t]
                w[t, at, :] = ws[t]

        @pl.loop(lo, hi, unroll=2)
        def _(c):
            row = pl.multiple_of(8 * c, 8)
            at = pl.ds(row, 8)
            for t in range(nt):
                gg = g[t, at, :]
                xx = x[t, at, :]
                z = (sp[t, at, :] - xx) + (
                    gg * (column_conv(u, t, row) - 4.0 * xx)
                    + r[t, at, :] * column_conv(w, t, row)
                )
                d[t, at, :] = c1 * d[t, at, :] + c2 * z

    half = SWEEPS // 2

    @pl.loop(0, half)
    def _(k):
        sweep(k, 1, n_ext - 1)

    @pl.loop(half, SWEEPS - 1)
    def _(k):
        sweep(k, 2, n_ext - 2)

    @pl.loop(2, n_ext - 2)
    def _(c):
        at = pl.ds(pl.multiple_of(8 * c, 8), 8)
        for t in range(nt):
            x[t, at, :] = x[t, at, :] + d[t, at, :]

    pot_copies = [
        pltpu.make_async_copy(
            x.at[t, HALO : HALO + rows], pot_h.at[:, t * 128 : (t + 1) * 128], sem_out.at[0, t]
        )
        for t in range(lt)
    ]
    for c in pot_copies:
        c.start()

    @pl.when(has_dn)
    def _():
        i_up.wait_recv()

    @pl.when(has_up)
    def _():
        i_dn.wait_recv()

    i_lf.wait_recv()
    i_rt.wait_recv()

    def drift(c):
        row = pl.multiple_of(8 * c, 8)
        at = pl.ds(row + HALO, 8)
        left, right = shifts([x[t, at, :] for t in range(nt)])
        de = [
            -0.5 * (x[t, pl.ds(row + HALO + 1, 8), :] - x[t, pl.ds(row + HALO - 1, 8), :])
            for t in range(lt)
        ]
        dn_ = [0.5 * (right[t] - left[t]) for t in range(lt)]
        return row, de, dn_

    mx[...] = jnp.zeros((8, 128), F32)

    @pl.loop(0, n_rt)
    def _(c):
        row, de, dn_ = drift(c)
        best = mx[...]
        for t in range(lt):
            best = jnp.maximum(best, jnp.abs(de[t]) + jnp.abs(dn_[t]))
        mx[...] = best

    lat_copies = []
    for o in range(1, nlat):
        lat_copies.append(
            pltpu.make_async_remote_copy(
                src_ref=mx, dst_ref=rx_lat.at[o - 1],
                send_sem=ss_lat.at[o - 1], recv_sem=rs_lat.at[o - 1],
                device_id=(lax.rem(me_lat + o, nlat), me_lon), device_id_type=MESH,
            )
        )
        lat_copies[-1].start()

    def fluxes(s, lo, hi):
        @pl.loop(lo, hi)
        def _(c):
            row, de, dn_ = drift(c)
            at = pl.ds(row + 8, 8)
            tiles = [ion[s, t, at, :] for t in range(lt)]
            tiles.append(
                jnp.where(lane < 64, ion_fr[s, pl.ds(row, 8), :], ion_fl[s, pl.ds(row, 8), :])
            )
            left, right = shifts(tiles)
            for t in range(lt):
                n = tiles[t]
                f = jnp.maximum(de[t], 0.0) * (n - left[t])
                f = f + jnp.minimum(de[t], 0.0) * (right[t] - n)
                f = f + jnp.maximum(dn_[t], 0.0) * (n - ion[s, t, pl.ds(row + 7, 8), :])
                f = f + jnp.minimum(dn_[t], 0.0) * (ion[s, t, pl.ds(row + 9, 8), :] - n)
                flux[s, t, pl.ds(row, 8), :] = f

    fluxes(0, 0, n_rt)
    fluxes(1, 0, n_rt)
    best = mx[...]
    for o in range(1, nlat):
        lat_copies[o - 1].wait_recv()
        best = jnp.maximum(best, rx_lat[o - 1])
    mx2[...] = best
    lon_copies = []
    for o in range(1, nlon):
        lon_copies.append(
            pltpu.make_async_remote_copy(
                src_ref=mx2, dst_ref=rx_lon.at[o - 1],
                send_sem=ss_lon.at[o - 1], recv_sem=rs_lon.at[o - 1],
                device_id=(me_lat, lax.rem(me_lon + o, nlon)), device_id_type=MESH,
            )
        )
        lon_copies[-1].start()
    fluxes(2, 0, n_rt)
    best = mx2[...]
    for o in range(1, nlon):
        lon_copies[o - 1].wait_recv()
        best = jnp.maximum(best, rx_lon[o - 1])
    best = jnp.max(best, axis=0, keepdims=True)
    best = jnp.max(best, axis=1, keepdims=True)
    step = jnp.broadcast_to(COURANT / (best + 1e-6), (8, 128))

    upd_copies = []
    for s in range(3):
        scale = MOBILITY[s] * step

        @pl.loop(0, n_rt)
        def _(c):
            row = pl.multiple_of(8 * c, 8)
            for t in range(lt):
                upd[s, t, pl.ds(row, 8), :] = (
                    ion[s, t, pl.ds(row + 8, 8), :] - scale * flux[s, t, pl.ds(row, 8), :]
                )

        for t in range(lt):
            c = pltpu.make_async_copy(
                upd.at[s, t], upd_h.at[s, :, t * 128 : (t + 1) * 128], sem_out.at[1 + s, t]
            )
            c.start()
            upd_copies.append(c)

    @pl.when(has_up)
    def _():
        for c in [n_up, i_up] + ups:
            c.wait_send()

    @pl.when(has_dn)
    def _():
        for c in [n_dn, i_dn] + dns:
            c.wait_send()

    for c in [i_lf, i_rt, e_lf, e_rt] + sig_copies + t_copies + lons + lat_copies + lon_copies:
        c.wait_send()
    for c in pot_copies + upd_copies:
        c.wait()


def solution(mesh):
    nlat, nlon = mesh.shape["lat"], mesh.shape["lon"]
    theta, first_list, second_list = chebyshev_factors()

    def shards(pedersen, hall_conductivity, east_wind, north_wind, ion_density):
        lev, rows, cols = pedersen.shape
        lt = cols // 128
        nt = lt + 1
        ext = rows + 2 * HALO
        vm = lambda *shape: pltpu.VMEM(shape, F32)
        dma = lambda *shape: pltpu.SemaphoreType.DMA(shape)
        coef = jnp.array([first_list, second_list], F32)
        anyspec = pl.BlockSpec(memory_space=pl.ANY)
        return pl.pallas_call(
            functools.partial(kernel, nlat, nlon, lev, rows, lt),
            out_shape=(
                jax.ShapeDtypeStruct((rows, cols), F32),
                jax.ShapeDtypeStruct((3, rows, cols), F32),
            ),
            in_specs=[pl.BlockSpec(memory_space=pltpu.SMEM)] + [anyspec] * 5,
            out_specs=(anyspec, anyspec),
            scratch_shapes=[vm(lev, rows, cols)] * 4
            + [vm(3, lt, rows + 16, 128), vm(3, rows, 128), vm(3, rows, 128)]
            + [vm(lt, rows, 128), vm(lt, rows, 128), vm(lt, rows + 16, 128)]
            + [vm(rows, 128)] * 2
            + [vm(lt, rows, 128)] * 4
            + [vm(nt, ext, 128)] * 2
            + [vm(ext, 128)] * 4
            + [vm(nt, ext, 128)] * 7
            + [vm(3, lt, rows, 128)] * 2
            + [vm(8, 128), vm(nlat - 1, 8, 128), vm(8, 128), vm(nlon - 1, 8, 128)]
            + [dma(rows // 8, 4), dma(3, lt), dma(4, lt), dma(26), dma(26)]
            + [dma(nlat - 1)] * 2
            + [dma(nlon - 1)] * 2,
            compiler_params=pltpu.CompilerParams(
                collective_id=0, has_side_effects=True, vmem_limit_bytes=60 * 1024 * 1024
            ),
        )(coef, pedersen, hall_conductivity, east_wind, north_wind, ion_density)

    spec = P(None, "lat", "lon")
    return jax.shard_map(
        shards,
        mesh=mesh,
        in_specs=(spec,) * 5,
        out_specs=(P("lat", "lon"), spec),
        check_vma=False,
    )
```

```python
import functools

import jax
import jax.numpy as jnp
from jax import lax
from jax.experimental import pallas as pl
from jax.experimental.pallas import tpu as pltpu
from jax.sharding import PartitionSpec as P

SWEEPS = 16
DAMPING = 0.0001
LOW_BOUND = 0.05
HIGH_BOUND = 2.0
COURANT = 0.8
MOBILITY = (1.0, 0.6, 0.3)
MESH = pl.DeviceIdType.MESH
HALO = 24
F32 = jnp.float32


def chebyshev_factors():
    theta = 0.5 * (HIGH_BOUND + LOW_BOUND)
    delta = 0.5 * (HIGH_BOUND - LOW_BOUND)
    sigma_one = theta / delta
    rho_prev = 1.0 / sigma_one
    first_list = []
    second_list = []
    for sweep in range(SWEEPS):
        rho_next = 1.0 / (2.0 * sigma_one - rho_prev)
        first_list.append(rho_next * rho_prev)
        second_list.append(2.0 * rho_next / delta)
        rho_prev = rho_next
    return (theta, first_list, second_list)


def unroll_of(count):
    return max(k for k in range(1, 11) if count % k == 0)


def kernel(
    nlat, nlon, lev, rows, lt,
    coef, ped_h, hall_h, east_h, north_h, ion_h,
    pot_h, upd_h,
    ped, hall, east, north,
    ion, ipk_l, ipk_r, ion_fr, ion_fl,
    sig, cur_e, cur_n, e_fr, e_fl, s_one, t_out, sig_rx, t_rx,
    S, src, pk_l, pk_r, rx_fr, rx_fl,
    g, r, sp, x, d, u, w,
    flux, mx, rx_lat, mx2, rx_lon,
    sem_in, sem_ion, ss, rs, ss_lat, rs_lat, ss_lon, rs_lon,
):
    n_rt = rows // 8
    nt = lt + 1
    me_lat = lax.axis_index("lat")
    me_lon = lax.axis_index("lon")
    has_up = me_lat > 0
    has_dn = me_lat < nlat - 1
    up = (jnp.maximum(me_lat - 1, 0), me_lon)
    dn = (jnp.minimum(me_lat + 1, nlat - 1), me_lon)
    lf = (me_lat, lax.rem(me_lon + nlon - 1, nlon))
    rt = (me_lat, lax.rem(me_lon + 1, nlon))
    mirror = (nlat - 1 - me_lat, me_lon)

    order = [0, n_rt - 1] + list(range(1, n_rt - 1))
    hbm_in = (ped_h, hall_h, east_h, north_h)
    vm_in = (ped, hall, east, north)

    def in_copy(a, row, slot):
        return pltpu.make_async_copy(
            hbm_in[a].at[:, pl.ds(row, 8), :], vm_in[a].at[:, pl.ds(row, 8), :], sem_in.at[slot, a]
        )

    def ion_copy(s, t):
        return pltpu.make_async_copy(
            ion_h.at[s, :, t * 128 : (t + 1) * 128], ion.at[s, t, 8 : 8 + rows], sem_ion.at[s, t]
        )

    for c in order[:2]:
        for a in range(4):
            in_copy(a, 8 * c, c).start()
    for s in range(3):
        for t in range(lt):
            ion_copy(s, t).start()
    for c in order[2:]:
        for a in range(4):
            in_copy(a, 8 * c, c).start()

    barrier = pltpu.get_barrier_semaphore()
    for o in range(1, nlat):
        pl.semaphore_signal(
            barrier, inc=1, device_id=(lax.rem(me_lat + o, nlat), me_lon), device_id_type=MESH
        )
    for o in range(1, nlon):
        pl.semaphore_signal(
            barrier, inc=1, device_id=(me_lat, lax.rem(me_lon + o, nlon)), device_id_type=MESH
        )
    pl.semaphore_wait(barrier, nlat + nlon - 2)

    def rcopy(src_ref, dst_ref, k, dev):
        return pltpu.make_async_remote_copy(
            src_ref=src_ref, dst_ref=dst_ref, send_sem=ss.at[k], recv_sem=rs.at[k],
            device_id=dev, device_id_type=MESH,
        )

    lane = lax.broadcasted_iota(jnp.int32, (8, 128), 1)
    sub = lax.broadcasted_iota(jnp.int32, (8, 128), 0)

    def shifts(v):
        m = len(v)
        a = [pltpu.roll(t, 1, 1) for t in v]
        b = [pltpu.roll(t, 127, 1) for t in v]
        left = [jnp.where(lane == 0, a[j - 1], a[j]) for j in range(m)]
        right = [jnp.where(lane == 127, b[(j + 1) % m], b[j]) for j in range(m)]
        return left, right

    def smooth(v):
        left, right = shifts(v)
        return [t + 0.5 * (p + q) for t, p, q in zip(v, left, right)]

    def rev8(v):
        v = pltpu.roll(v, 4, 0)
        for b in (2, 1):
            v = jnp.where((sub & b) == 0, pltpu.roll(v, 8 - b, 0), pltpu.roll(v, b, 0))
        return v

    weight = [(0.5 + l / lev) / lev for l in range(lev)]

    def columns(c):
        row = pl.multiple_of(8 * c, 8)
        for a in range(4):
            in_copy(a, row, c).wait()
        for t in range(lt):
            at = (pl.ds(row, 8), slice(t * 128, (t + 1) * 128))
            acc = [jnp.zeros((8, 128), F32)] * 3
            for l in range(lev):
                p, h = weight[l] * ped[(l,) + at], weight[l] * hall[(l,) + at]
                e, n = east[(l,) + at], north[(l,) + at]
                acc = [acc[0] + p, acc[1] + (p * e + h * n), acc[2] + (p * n - h * e)]
            sig[t, pl.ds(row, 8), :] = acc[0]
            cur_e[t, pl.ds(row, 8), :] = acc[1]
            cur_n[t, pl.ds(row + 8, 8), :] = acc[2]

    def both(lo, hi):
        @pl.loop(lo, hi)
        def _(c):
            columns(c)

    both(0, 1)
    both(n_rt - 1, n_rt)
    n_up = rcopy(cur_n.at[:, 8:16], cur_n.at[:, rows + 8 : rows + 16], 0, up)
    n_dn = rcopy(cur_n.at[:, rows : rows + 8], cur_n.at[:, 0:8], 1, dn)
    i_up = rcopy(ion.at[:, :, 8:16], ion.at[:, :, rows + 8 : rows + 16], 2, up)
    i_dn = rcopy(ion.at[:, :, rows : rows + 8], ion.at[:, :, 0:8], 3, dn)
    i_lf = rcopy(ipk_l, ion_fr, 4, lf)
    i_rt = rcopy(ipk_r, ion_fl, 5, rt)

    for s in range(3):
        for t in range(lt):
            ion_copy(s, t).wait()

    @pl.when(has_up)
    def _():
        n_up.start()
        i_up.start()

    @pl.when(has_dn)
    def _():
        n_dn.start()
        i_dn.start()

    @pl.when(jnp.logical_not(has_up))
    def _():
        cur_n[:, 0:8, :] = jnp.zeros((lt, 8, 128), F32)
        ion[:, :, 0:8, :] = jnp.zeros((3, lt, 8, 128), F32)

    @pl.when(jnp.logical_not(has_dn))
    def _():
        cur_n[:, rows + 8 : rows + 16, :] = jnp.zeros((lt, 8, 128), F32)
        ion[:, :, rows + 8 : rows + 16, :] = jnp.zeros((3, lt, 8, 128), F32)

    pieces = 4
    per = n_rt // pieces
    sig_copies = []
    for q in range(pieces):
        both(max(1, q * per), min(n_rt - 1, (q + 1) * per))
        band = slice(q * per * 8, (q + 1) * per * 8)
        copy = rcopy(sig.at[:, band], sig_rx.at[:, band], 6 + q, mirror)
        copy.start()
        sig_copies.append(copy)

    e_lf = rcopy(cur_e.at[0], e_fr, 10, lf)
    e_rt = rcopy(cur_e.at[lt - 1], e_fl, 11, rt)
    e_lf.start()
    e_rt.start()

    @pl.loop(0, n_rt)
    def _(c):
        at = pl.ds(pl.multiple_of(8 * c, 8), 8)
        inner = pl.ds(pl.multiple_of(8 * c + 8, 8), 8)
        a, b = [], []
        for s in range(3):
            v, q = ion[s, 0, inner, :], ion[s, lt - 1, inner, :]
            a.append(pltpu.roll(v, 32 * s, 1) if s else v)
            b.append(pltpu.roll(q, 32 * (s + 1), 1))
        ipk_l[at, :] = jnp.where(lane < 32, a[0], jnp.where(lane < 64, a[1], a[2]))
        ipk_r[at, :] = jnp.where(lane < 32, b[0], jnp.where(lane < 64, b[1], b[2]))

    i_lf.start()
    i_rt.start()

    @pl.when(has_dn)
    def _():
        n_up.wait_recv()

    @pl.when(has_up)
    def _():
        n_dn.wait_recv()

    e_lf.wait_recv()
    e_rt.wait_recv()

    t_copies = []
    for q in range(pieces):
        @pl.loop(q * per, (q + 1) * per)
        def _(c):
            row = pl.multiple_of(8 * c, 8)
            tiles = [cur_e[t, pl.ds(row, 8), :] for t in range(lt)]
            tiles.append(jnp.where(lane < 64, e_fr[pl.ds(row, 8), :], e_fl[pl.ds(row, 8), :]))
            left, right = shifts(tiles)
            for t in range(lt):
                d_lon = 0.5 * (right[t] - left[t])
                d_lat = 0.5 * (cur_n[t, pl.ds(row + 9, 8), :] - cur_n[t, pl.ds(row + 7, 8), :])
                s_one[t, pl.ds(row, 8), :] = d_lon + d_lat
                t_out[t, pl.ds(row, 8), :] = d_lon - d_lat

        band = slice(q * per * 8, (q + 1) * per * 8)
        copy = rcopy(t_out.at[:, band], t_rx.at[:, band], 12 + q, mirror)
        copy.start()
        t_copies.append(copy)

    def zero_rows(ref, lo, hi):
        ref[0:lt, lo:hi, :] = jnp.zeros((lt, hi - lo, 128), F32)

    @pl.when(jnp.logical_not(has_up))
    def _():
        zero_rows(S, 0, HALO)
        zero_rows(src, 0, HALO)

    @pl.when(jnp.logical_not(has_dn))
    def _():
        zero_rows(S, HALO + rows, 2 * HALO + rows)
        zero_rows(src, HALO + rows, 2 * HALO + rows)

    def combine(own, rx, out, q):
        @pl.loop((pieces - 1 - q) * per, (pieces - q) * per)
        def _(c):
            row = pl.multiple_of(8 * c, 8)
            back = pl.multiple_of(rows - 8 - 8 * c, 8)
            for t in range(lt):
                out[t, pl.ds(row + HALO, 8), :] = own[t, pl.ds(row, 8), :] + rev8(
                    rx[t, pl.ds(back, 8), :]
                )

    for q in range(pieces):
        sig_copies[q].wait_recv()
        combine(sig, sig_rx, S, q)
    for q in range(pieces):
        t_copies[q].wait_recv()
        combine(s_one, t_rx, src, q)

    lo_in, lo_out = slice(HALO, 2 * HALO), slice(0, HALO)
    hi_in, hi_out = slice(rows, rows + HALO), slice(rows + HALO, rows + 2 * HALO)
    mid = slice(HALO, HALO + rows)
    ups = [
        rcopy(f.at[0:lt, lo_in], f.at[0:lt, hi_out], 16 + k, up) for k, f in enumerate((S, src))
    ]
    dns = [
        rcopy(f.at[0:lt, hi_in], f.at[0:lt, lo_out], 18 + k, dn) for k, f in enumerate((S, src))
    ]

    @pl.when(has_up)
    def _():
        for c in ups:
            c.start()

    @pl.when(has_dn)
    def _():
        for c in dns:
            c.start()

    def pack(lo, hi):
        @pl.loop(lo // 8, hi // 8)
        def _(c):
            at = pl.ds(pl.multiple_of(8 * c, 8), 8)
            pk_l[at, :] = jnp.where(lane < 64, S[0, at, :], pltpu.roll(src[0, at, :], 64, 1))
            pk_r[at, :] = jnp.where(
                lane >= 64, S[lt - 1, at, :], pltpu.roll(src[lt - 1, at, :], 64, 1)
            )

    lons = []

    def send_lon(part, k):
        lons.append(rcopy(pk_l.at[part], rx_fr.at[part], k, lf))
        lons.append(rcopy(pk_r.at[part], rx_fl.at[part], k + 1, rt))
        lons[-2].start()
        lons[-1].start()

    pack(HALO, HALO + rows)
    send_lon(mid, 20)

    @pl.when(has_up)
    def _():
        for c in dns:
            c.wait_recv()

    pack(0, HALO)
    send_lon(lo_out, 22)

    @pl.when(has_dn)
    def _():
        for c in ups:
            c.wait_recv()

    pack(HALO + rows, 2 * HALO + rows)
    send_lon(hi_out, 24)
    for c in lons:
        c.wait_recv()

    n_ext = (rows + 2 * HALO) // 8
    total = rows * nlat

    @pl.loop(0, n_ext)
    def _(c):
        at = pl.ds(pl.multiple_of(8 * c, 8), 8)
        fr, fl = rx_fr[at, :], rx_fl[at, :]
        s_halo = jnp.where(lane < 64, fr, fl)
        S[lt, at, :] = s_halo
        src[lt, at, :] = pltpu.roll(jnp.where(lane >= 64, fr, fl), 64, 1)
        tiles = [S[t, at, :] for t in range(lt)] + [s_halo]
        for t, v in enumerate(smooth(tiles)):
            u[t, at, :] = v
            w[t, at, :] = jnp.zeros((8, 128), F32)

    theta = 0.5 * (HIGH_BOUND + LOW_BOUND)

    def column_conv(ref, t, row):
        return (
            ref[t, pl.ds(row - 1, 8), :] + ref[t, pl.ds(row + 1, 8), :]
        ) + 2.0 * ref[t, pl.ds(row, 8), :]

    @pl.loop(1, n_ext - 1)
    def _(c):
        row = pl.multiple_of(8 * c, 8)
        at = pl.ds(row, 8)
        where = sub + (row - HALO + me_lat * rows)
        inside = (where >= 0) & (where < total)
        for t in range(nt):
            s = S[t, at, :]
            diag = DAMPING + 0.5 * (4.0 * s + column_conv(u, t, row))
            inv = jnp.where(inside, 1.0 / diag, 0.0)
            half = 0.5 * inv
            r[t, at, :] = half
            g[t, at, :] = half * s
            first = src[t, at, :] * inv
            sp[t, at, :] = first
            d[t, at, :] = first * (1.0 / theta)
            x[t, at, :] = jnp.zeros((8, 128), F32)

    def sweep(k, lo, hi):
        c1 = coef[0, k]
        c2 = coef[1, k]

        @pl.loop(lo, hi, unroll=unroll_of(hi - lo))
        def _(c):
            at = pl.ds(pl.multiple_of(8 * c, 8), 8)
            xs = [x[t, at, :] + d[t, at, :] for t in range(nt)]
            ys = [S[t, at, :] * xs[t] for t in range(nt)]
            us = smooth(xs)
            ws = smooth(ys)
            for t in range(nt):
                x[t, at, :] = xs[t]
                u[t, at, :] = us[t]
                w[t, at, :] = ws[t]

        @pl.loop(lo, hi, unroll=unroll_of(hi - lo))
        def _(c):
            row = pl.multiple_of(8 * c, 8)
            at = pl.ds(row, 8)
            for t in range(nt):
                gg = g[t, at, :]
                xx = x[t, at, :]
                z = (sp[t, at, :] - xx) + (
                    gg * (column_conv(u, t, row) - 4.0 * xx)
                    + r[t, at, :] * column_conv(w, t, row)
                )
                d[t, at, :] = c1 * d[t, at, :] + c2 * z

    half = SWEEPS // 2

    @pl.loop(0, half)
    def _(k):
        sweep(k, 1, n_ext - 1)

    @pl.loop(half, SWEEPS - 1)
    def _(k):
        sweep(k, 2, n_ext - 2)

    @pl.loop(2, n_ext - 2)
    def _(c):
        at = pl.ds(pl.multiple_of(8 * c, 8), 8)
        for t in range(nt):
            x[t, at, :] = x[t, at, :] + d[t, at, :]

    @pl.loop(0, n_rt)
    def _(c):
        row = pl.multiple_of(8 * c, 8)
        for t in range(lt):
            pot_h[pl.ds(row, 8), t * 128 : (t + 1) * 128] = x[t, pl.ds(row + HALO, 8), :]

    @pl.when(has_dn)
    def _():
        i_up.wait_recv()

    @pl.when(has_up)
    def _():
        i_dn.wait_recv()

    i_lf.wait_recv()
    i_rt.wait_recv()

    def drift(c):
        row = pl.multiple_of(8 * c, 8)
        at = pl.ds(row + HALO, 8)
        left, right = shifts([x[t, at, :] for t in range(nt)])
        de = [
            -0.5 * (x[t, pl.ds(row + HALO + 1, 8), :] - x[t, pl.ds(row + HALO - 1, 8), :])
            for t in range(lt)
        ]
        dn_ = [0.5 * (right[t] - left[t]) for t in range(lt)]
        return row, de, dn_

    mx[...] = jnp.zeros((8, 128), F32)

    @pl.loop(0, n_rt)
    def _(c):
        row, de, dn_ = drift(c)
        best = mx[...]
        for t in range(lt):
            best = jnp.maximum(best, jnp.abs(de[t]) + jnp.abs(dn_[t]))
        mx[...] = best

    lat_copies = []
    for o in range(1, nlat):
        lat_copies.append(
            pltpu.make_async_remote_copy(
                src_ref=mx, dst_ref=rx_lat.at[o - 1],
                send_sem=ss_lat.at[o - 1], recv_sem=rs_lat.at[o - 1],
                device_id=(lax.rem(me_lat + o, nlat), me_lon), device_id_type=MESH,
            )
        )
        lat_copies[-1].start()

    def fluxes(s, lo, hi):
        @pl.loop(lo, hi)
        def _(c):
            row, de, dn_ = drift(c)
            at = pl.ds(row + 8, 8)
            tiles = [ion[s, t, at, :] for t in range(lt)]
            tiles.append(
                jnp.where(
                    lane < 64,
                    pltpu.roll(ion_fr[pl.ds(row, 8), :], (128 - 32 * s) % 128, 1),
                    pltpu.roll(ion_fl[pl.ds(row, 8), :], 96 - 32 * s, 1),
                )
            )
            left, right = shifts(tiles)
            for t in range(lt):
                n = tiles[t]
                f = jnp.maximum(de[t], 0.0) * (n - left[t])
                f = f + jnp.minimum(de[t], 0.0) * (right[t] - n)
                f = f + jnp.maximum(dn_[t], 0.0) * (n - ion[s, t, pl.ds(row + 7, 8), :])
                f = f + jnp.minimum(dn_[t], 0.0) * (ion[s, t, pl.ds(row + 9, 8), :] - n)
                flux[s, t, pl.ds(row, 8), :] = f

    fluxes(0, 0, n_rt)
    fluxes(1, 0, n_rt)
    best = mx[...]
    for o in range(1, nlat):
        lat_copies[o - 1].wait_recv()
        best = jnp.maximum(best, rx_lat[o - 1])
    mx2[...] = best
    lon_copies = []
    for o in range(1, nlon):
        lon_copies.append(
            pltpu.make_async_remote_copy(
                src_ref=mx2, dst_ref=rx_lon.at[o - 1],
                send_sem=ss_lon.at[o - 1], recv_sem=rs_lon.at[o - 1],
                device_id=(me_lat, lax.rem(me_lon + o, nlon)), device_id_type=MESH,
            )
        )
        lon_copies[-1].start()
    fluxes(2, 0, n_rt)
    best = mx2[...]
    for o in range(1, nlon):
        lon_copies[o - 1].wait_recv()
        best = jnp.maximum(best, rx_lon[o - 1])
    best = jnp.max(best, axis=0, keepdims=True)
    best = jnp.max(best, axis=1, keepdims=True)
    step = jnp.broadcast_to(COURANT / (best + 1e-6), (8, 128))

    for s in range(3):
        scale = MOBILITY[s] * step

        @pl.loop(0, n_rt)
        def _(c):
            row = pl.multiple_of(8 * c, 8)
            for t in range(lt):
                upd_h[s, pl.ds(row, 8), t * 128 : (t + 1) * 128] = (
                    ion[s, t, pl.ds(row + 8, 8), :] - scale * flux[s, t, pl.ds(row, 8), :]
                )

    @pl.when(has_up)
    def _():
        for c in [n_up, i_up] + ups:
            c.wait_send()

    @pl.when(has_dn)
    def _():
        for c in [n_dn, i_dn] + dns:
            c.wait_send()

    for c in [i_lf, i_rt, e_lf, e_rt] + sig_copies + t_copies + lons + lat_copies + lon_copies:
        c.wait_send()


def solution(mesh):
    nlat, nlon = mesh.shape["lat"], mesh.shape["lon"]
    theta, first_list, second_list = chebyshev_factors()

    def shards(pedersen, hall_conductivity, east_wind, north_wind, ion_density):
        lev, rows, cols = pedersen.shape
        lt = cols // 128
        nt = lt + 1
        ext = rows + 2 * HALO
        vm = lambda *shape: pltpu.VMEM(shape, F32)
        dma = lambda *shape: pltpu.SemaphoreType.DMA(shape)
        coef = jnp.array([first_list, second_list], F32)
        anyspec = pl.BlockSpec(memory_space=pl.ANY)
        return pl.pallas_call(
            functools.partial(kernel, nlat, nlon, lev, rows, lt),
            out_shape=(
                jax.ShapeDtypeStruct((rows, cols), F32),
                jax.ShapeDtypeStruct((3, rows, cols), F32),
            ),
            in_specs=[pl.BlockSpec(memory_space=pltpu.SMEM)] + [anyspec] * 5,
            out_specs=(pl.BlockSpec(memory_space=pltpu.VMEM),) * 2,
            scratch_shapes=[vm(lev, rows, cols)] * 4
            + [vm(3, lt, rows + 16, 128), vm(rows, 128), vm(rows, 128)] + [vm(rows, 128)] * 2
            + [vm(lt, rows, 128), vm(lt, rows, 128), vm(lt, rows + 16, 128)]
            + [vm(rows, 128)] * 2
            + [vm(lt, rows, 128)] * 4
            + [vm(nt, ext, 128)] * 2
            + [vm(ext, 128)] * 4
            + [vm(nt, ext, 128)] * 7
            + [vm(3, lt, rows, 128)]
            + [vm(8, 128), vm(nlat - 1, 8, 128), vm(8, 128), vm(nlon - 1, 8, 128)]
            + [dma(rows // 8, 4), dma(3, lt), dma(26), dma(26)]
            + [dma(nlat - 1)] * 2
            + [dma(nlon - 1)] * 2,
            compiler_params=pltpu.CompilerParams(
                collective_id=0, has_side_effects=True, vmem_limit_bytes=60 * 1024 * 1024
            ),
        )(coef, pedersen, hall_conductivity, east_wind, north_wind, ion_density)

    spec = P(None, "lat", "lon")
    return jax.shard_map(
        shards,
        mesh=mesh,
        in_specs=(spec,) * 5,
        out_specs=(P("lat", "lon"), spec),
        check_vma=False,
    )
```

```python
import functools

import jax
import jax.numpy as jnp
from jax import lax
from jax.experimental import pallas as pl
from jax.experimental.pallas import tpu as pltpu
from jax.sharding import PartitionSpec as P

SWEEPS = 16
DAMPING = 0.0001
LOW_BOUND = 0.05
HIGH_BOUND = 2.0
COURANT = 0.8
MOBILITY = (1.0, 0.6, 0.3)
MESH = pl.DeviceIdType.MESH
HALO = 24
F32 = jnp.float32


def chebyshev_factors():
    theta = 0.5 * (HIGH_BOUND + LOW_BOUND)
    delta = 0.5 * (HIGH_BOUND - LOW_BOUND)
    sigma_one = theta / delta
    rho_prev = 1.0 / sigma_one
    first_list = []
    second_list = []
    for sweep in range(SWEEPS):
        rho_next = 1.0 / (2.0 * sigma_one - rho_prev)
        first_list.append(rho_next * rho_prev)
        second_list.append(2.0 * rho_next / delta)
        rho_prev = rho_next
    return (theta, first_list, second_list)


def unroll_of(count):
    return max(k for k in range(1, 11) if count % k == 0)


def kernel(
    nlat, nlon, lev, rows, lt,
    coef, ped_h, hall_h, east_h, north_h, ion_h,
    pot_h, upd_h,
    ped, hall, east, north,
    ion, ipk_l, ipk_r, ion_fr, ion_fl,
    sig, cur_e, cur_n, e_fr, e_fl, s_one, t_out, sig_rx, t_rx,
    S, src, SS, lhs, to_strided, to_plain, xn, pk_l, pk_r, rx_fr, rx_fl,
    g, r, sp, x, d, u, w,
    flux, mx, rx_lat, mx2, rx_lon,
    sem_in, sem_ion, ss, rs, ss_lat, rs_lat, ss_lon, rs_lon,
):
    n_rt = rows // 8
    nt = lt + 1
    me_lat = lax.axis_index("lat")
    me_lon = lax.axis_index("lon")
    has_up = me_lat > 0
    has_dn = me_lat < nlat - 1
    up = (jnp.maximum(me_lat - 1, 0), me_lon)
    dn = (jnp.minimum(me_lat + 1, nlat - 1), me_lon)
    lf = (me_lat, lax.rem(me_lon + nlon - 1, nlon))
    rt = (me_lat, lax.rem(me_lon + 1, nlon))
    mirror = (nlat - 1 - me_lat, me_lon)

    order = [0, n_rt - 1] + list(range(1, n_rt - 1))
    hbm_in = (ped_h, hall_h, east_h, north_h)
    vm_in = (ped, hall, east, north)

    def in_copy(a, row, slot):
        return pltpu.make_async_copy(
            hbm_in[a].at[:, pl.ds(row, 8), :], vm_in[a].at[:, pl.ds(row, 8), :], sem_in.at[slot, a]
        )

    def ion_copy(s, t):
        return pltpu.make_async_copy(
            ion_h.at[s, :, t * 128 : (t + 1) * 128], ion.at[s, t, 8 : 8 + rows], sem_ion.at[s, t]
        )

    for c in order[:2]:
        for a in range(4):
            in_copy(a, 8 * c, c).start()
    for s in range(3):
        for t in range(lt):
            ion_copy(s, t).start()
    for c in order[2:]:
        for a in range(4):
            in_copy(a, 8 * c, c).start()

    barrier = pltpu.get_barrier_semaphore()
    for o in range(1, nlat):
        pl.semaphore_signal(
            barrier, inc=1, device_id=(lax.rem(me_lat + o, nlat), me_lon), device_id_type=MESH
        )
    for o in range(1, nlon):
        pl.semaphore_signal(
            barrier, inc=1, device_id=(me_lat, lax.rem(me_lon + o, nlon)), device_id_type=MESH
        )
    pl.semaphore_wait(barrier, nlat + nlon - 2)

    def rcopy(src_ref, dst_ref, k, dev):
        return pltpu.make_async_remote_copy(
            src_ref=src_ref, dst_ref=dst_ref, send_sem=ss.at[k], recv_sem=rs.at[k],
            device_id=dev, device_id_type=MESH,
        )

    lane = lax.broadcasted_iota(jnp.int32, (8, 128), 1)
    sub = lax.broadcasted_iota(jnp.int32, (8, 128), 0)

    def shifts(v):
        m = len(v)
        a = [pltpu.roll(t, 1, 1) for t in v]
        b = [pltpu.roll(t, 127, 1) for t in v]
        left = [jnp.where(lane == 0, a[j - 1], a[j]) for j in range(m)]
        right = [jnp.where(lane == 127, b[(j + 1) % m], b[j]) for j in range(m)]
        return left, right

    def rev8(v):
        v = pltpu.roll(v, 4, 0)
        for b in (2, 1):
            v = jnp.where((sub & b) == 0, pltpu.roll(v, 8 - b, 0), pltpu.roll(v, b, 0))
        return v

    weight = [(0.5 + l / lev) / lev for l in range(lev)]

    def columns(c):
        row = pl.multiple_of(8 * c, 8)
        for a in range(4):
            in_copy(a, row, c).wait()
        for t in range(lt):
            at = (pl.ds(row, 8), slice(t * 128, (t + 1) * 128))
            acc = [jnp.zeros((8, 128), F32)] * 3
            for l in range(lev):
                p, h = weight[l] * ped[(l,) + at], weight[l] * hall[(l,) + at]
                e, n = east[(l,) + at], north[(l,) + at]
                acc = [acc[0] + p, acc[1] + (p * e + h * n), acc[2] + (p * n - h * e)]
            sig[t, pl.ds(row, 8), :] = acc[0]
            cur_e[t, pl.ds(row, 8), :] = acc[1]
            cur_n[t, pl.ds(row + 8, 8), :] = acc[2]

    def both(lo, hi):
        @pl.loop(lo, hi)
        def _(c):
            columns(c)

    both(0, 1)
    both(n_rt - 1, n_rt)
    n_up = rcopy(cur_n.at[:, 8:16], cur_n.at[:, rows + 8 : rows + 16], 0, up)
    n_dn = rcopy(cur_n.at[:, rows : rows + 8], cur_n.at[:, 0:8], 1, dn)
    i_up = rcopy(ion.at[:, :, 8:16], ion.at[:, :, rows + 8 : rows + 16], 2, up)
    i_dn = rcopy(ion.at[:, :, rows : rows + 8], ion.at[:, :, 0:8], 3, dn)
    i_lf = rcopy(ipk_l, ion_fr, 4, lf)
    i_rt = rcopy(ipk_r, ion_fl, 5, rt)

    for s in range(3):
        for t in range(lt):
            ion_copy(s, t).wait()

    @pl.when(has_up)
    def _():
        n_up.start()
        i_up.start()

    @pl.when(has_dn)
    def _():
        n_dn.start()
        i_dn.start()

    @pl.when(jnp.logical_not(has_up))
    def _():
        cur_n[:, 0:8, :] = jnp.zeros((lt, 8, 128), F32)
        ion[:, :, 0:8, :] = jnp.zeros((3, lt, 8, 128), F32)

    @pl.when(jnp.logical_not(has_dn))
    def _():
        cur_n[:, rows + 8 : rows + 16, :] = jnp.zeros((lt, 8, 128), F32)
        ion[:, :, rows + 8 : rows + 16, :] = jnp.zeros((3, lt, 8, 128), F32)

    pieces = 4
    per = n_rt // pieces
    sig_copies = []
    for q in range(pieces):
        both(max(1, q * per), min(n_rt - 1, (q + 1) * per))
        band = slice(q * per * 8, (q + 1) * per * 8)
        copy = rcopy(sig.at[:, band], sig_rx.at[:, band], 6 + q, mirror)
        copy.start()
        sig_copies.append(copy)

    e_lf = rcopy(cur_e.at[0], e_fr, 10, lf)
    e_rt = rcopy(cur_e.at[lt - 1], e_fl, 11, rt)
    e_lf.start()
    e_rt.start()

    @pl.loop(0, n_rt)
    def _(c):
        at = pl.ds(pl.multiple_of(8 * c, 8), 8)
        inner = pl.ds(pl.multiple_of(8 * c + 8, 8), 8)
        a, b = [], []
        for s in range(3):
            v, q = ion[s, 0, inner, :], ion[s, lt - 1, inner, :]
            a.append(pltpu.roll(v, 32 * s, 1) if s else v)
            b.append(pltpu.roll(q, 32 * (s + 1), 1))
        ipk_l[at, :] = jnp.where(lane < 32, a[0], jnp.where(lane < 64, a[1], a[2]))
        ipk_r[at, :] = jnp.where(lane < 32, b[0], jnp.where(lane < 64, b[1], b[2]))

    i_lf.start()
    i_rt.start()

    @pl.when(has_dn)
    def _():
        n_up.wait_recv()

    @pl.when(has_up)
    def _():
        n_dn.wait_recv()

    e_lf.wait_recv()
    e_rt.wait_recv()

    t_copies = []
    for q in [0, pieces - 1] + list(range(1, pieces - 1)):
        @pl.loop(q * per, (q + 1) * per)
        def _(c):
            row = pl.multiple_of(8 * c, 8)
            tiles = [cur_e[t, pl.ds(row, 8), :] for t in range(lt)]
            tiles.append(jnp.where(lane < 64, e_fr[pl.ds(row, 8), :], e_fl[pl.ds(row, 8), :]))
            left, right = shifts(tiles)
            for t in range(lt):
                d_lon = 0.5 * (right[t] - left[t])
                d_lat = 0.5 * (cur_n[t, pl.ds(row + 9, 8), :] - cur_n[t, pl.ds(row + 7, 8), :])
                s_one[t, pl.ds(row, 8), :] = d_lon + d_lat
                t_out[t, pl.ds(row, 8), :] = d_lon - d_lat

        band = slice(q * per * 8, (q + 1) * per * 8)
        copy = rcopy(t_out.at[:, band], t_rx.at[:, band], 12 + q, mirror)
        copy.start()
        t_copies.append((q, copy))

    width = nt * 128

    @pl.loop(0, width // 16)
    def _(c):
        row = lax.broadcasted_iota(jnp.int32, (16, 128), 0) + 16 * c
        col = lax.broadcasted_iota(jnp.int32, (16, 128), 1)
        for t in range(nt):
            there = jnp.where(row == col * nt + t, 1.0, 0.0).astype(jnp.bfloat16)
            for part in range(3):
                at = pl.ds(pl.multiple_of(part * width + 16 * c, 16), 16)
                to_strided[at, t * 128 : (t + 1) * 128] = there

    for j in range(nt):
        @pl.loop(0, 8)
        def _(c):
            row = lax.broadcasted_iota(jnp.int32, (16, 128), 0) + 16 * c
            col = lax.broadcasted_iota(jnp.int32, (16, 128), 1)
            for t in range(nt):
                back = jnp.where(row * nt + j == col + t * 128, 1.0, 0.0).astype(jnp.bfloat16)
                for part in range(3):
                    at = pl.ds(pl.multiple_of(part * width + j * 128 + 16 * c, 16), 16)
                    to_plain[at, t * 128 : (t + 1) * 128] = back

    def split(v, at, t):
        for part in range(3):
            low = v.astype(jnp.bfloat16)
            lhs[at, part * width + t * 128 : part * width + (t + 1) * 128] = low
            v = v - low.astype(F32)

    def zero_rows(ref, lo, hi):
        ref[0:lt, lo:hi, :] = jnp.zeros((lt, hi - lo, 128), F32)

    @pl.when(jnp.logical_not(has_up))
    def _():
        zero_rows(S, 0, HALO)
        zero_rows(src, 0, HALO)

    @pl.when(jnp.logical_not(has_dn))
    def _():
        zero_rows(S, HALO + rows, 2 * HALO + rows)
        zero_rows(src, HALO + rows, 2 * HALO + rows)

    def combine(own, rx, out, q):
        @pl.loop((pieces - 1 - q) * per, (pieces - q) * per)
        def _(c):
            row = pl.multiple_of(8 * c, 8)
            back = pl.multiple_of(rows - 8 - 8 * c, 8)
            for t in range(lt):
                out[t, pl.ds(row + HALO, 8), :] = own[t, pl.ds(row, 8), :] + rev8(
                    rx[t, pl.ds(back, 8), :]
                )

    for q in range(pieces):
        sig_copies[q].wait_recv()
        combine(sig, sig_rx, S, q)
    lo_in, lo_out = slice(HALO, 2 * HALO), slice(0, HALO)
    hi_in, hi_out = slice(rows, rows + HALO), slice(rows + HALO, rows + 2 * HALO)
    ups = [
        rcopy(f.at[0:lt, lo_in], f.at[0:lt, hi_out], 16 + k, up) for k, f in enumerate((S, src))
    ]
    dns = [
        rcopy(f.at[0:lt, hi_in], f.at[0:lt, lo_out], 18 + k, dn) for k, f in enumerate((S, src))
    ]

    def pack(lo, hi):
        @pl.loop(lo // 8, hi // 8)
        def _(c):
            at = pl.ds(pl.multiple_of(8 * c, 8), 8)
            pk_l[at, :] = jnp.where(lane < 64, S[0, at, :], pltpu.roll(src[0, at, :], 64, 1))
            pk_r[at, :] = jnp.where(
                lane >= 64, S[lt - 1, at, :], pltpu.roll(src[lt - 1, at, :], 64, 1)
            )

    lons = []

    def send_lon(part, k):
        lons.append(rcopy(pk_l.at[part], rx_fr.at[part], k, lf))
        lons.append(rcopy(pk_r.at[part], rx_fl.at[part], k + 1, rt))
        lons[-2].start()
        lons[-1].start()

    for i, (q, copy) in enumerate(t_copies):
        copy.wait_recv()
        combine(s_one, t_rx, src, q)
        if i == 1:
            @pl.when(has_up)
            def _():
                for c in ups:
                    c.start()

            @pl.when(has_dn)
            def _():
                for c in dns:
                    c.start()

        lo = HALO + (pieces - 1 - q) * per * 8
        pack(lo, lo + per * 8)
        send_lon(slice(lo, lo + per * 8), 20 + 2 * i)

    @pl.when(has_up)
    def _():
        for c in dns:
            c.wait_recv()

    pack(0, HALO)
    send_lon(lo_out, 28)

    @pl.when(has_dn)
    def _():
        for c in ups:
            c.wait_recv()

    pack(HALO + rows, 2 * HALO + rows)
    send_lon(hi_out, 30)
    for c in lons:
        c.wait_recv()

    n_ext = (rows + 2 * HALO) // 8
    total = rows * nlat

    lane16 = lax.broadcasted_iota(jnp.int32, (16, 128), 1)
    ext = 8 * n_ext

    @pl.loop(0, n_ext // 2)
    def _(c):
        row = pl.multiple_of(16 * c, 16)
        at = pl.ds(row, 16)
        at2 = pl.ds(pl.multiple_of(row + ext, 16), 16)
        fr, fl = rx_fr[at, :], rx_fl[at, :]
        for t in range(lt):
            split(S[t, at, :], at, t)
            split(src[t, at, :], at2, t)
        split(jnp.where(lane16 < 64, fr, fl), at, lt)
        split(pltpu.roll(jnp.where(lane16 >= 64, fr, fl), 64, 1), at2, lt)

    for f, out in enumerate((SS, sp)):
        moved = jnp.dot(
            lhs[f * ext : (f + 1) * ext, :], to_strided[...], preferred_element_type=F32
        )
        for t in range(nt):
            out[t, :, :] = moved[:, t * 128 : (t + 1) * 128]

    def smooth_strided(v):
        left = [pltpu.roll(v[-1], 1, 1)] + v[:-1]
        right = v[1:] + [pltpu.roll(v[0], 127, 1)]
        return [t + 0.5 * (p + q) for t, p, q in zip(v, left, right)]

    @pl.loop(0, n_ext)
    def _(c):
        at = pl.ds(pl.multiple_of(8 * c, 8), 8)
        for t, v in enumerate(smooth_strided([SS[t, at, :] for t in range(nt)])):
            u[t, at, :] = v
            w[t, at, :] = jnp.zeros((8, 128), F32)

    theta = 0.5 * (HIGH_BOUND + LOW_BOUND)

    def column_conv(ref, t, row):
        return (
            ref[t, pl.ds(row - 1, 8), :] + ref[t, pl.ds(row + 1, 8), :]
        ) + 2.0 * ref[t, pl.ds(row, 8), :]

    @pl.loop(1, n_ext - 1)
    def _(c):
        row = pl.multiple_of(8 * c, 8)
        at = pl.ds(row, 8)
        where = sub + (row - HALO + me_lat * rows)
        inside = (where >= 0) & (where < total)
        for t in range(nt):
            s = SS[t, at, :]
            diag = DAMPING + 0.5 * (4.0 * s + column_conv(u, t, row))
            inv = jnp.where(inside, 1.0 / diag, 0.0)
            half = 0.5 * inv
            r[t, at, :] = half
            g[t, at, :] = half * s
            first = sp[t, at, :] * inv
            sp[t, at, :] = first
            d[t, at, :] = first * (1.0 / theta)
            x[t, at, :] = jnp.zeros((8, 128), F32)

    def sweep(k, lo, hi):
        c1 = coef[0, k]
        c2 = coef[1, k]

        @pl.loop(lo, hi, unroll=unroll_of(hi - lo))
        def _(c):
            at = pl.ds(pl.multiple_of(8 * c, 8), 8)
            xs = [x[t, at, :] + d[t, at, :] for t in range(nt)]
            ys = [SS[t, at, :] * xs[t] for t in range(nt)]
            us = smooth_strided(xs)
            ws = smooth_strided(ys)
            for t in range(nt):
                x[t, at, :] = xs[t]
                u[t, at, :] = us[t]
                w[t, at, :] = ws[t]

        @pl.loop(lo, hi, unroll=unroll_of(hi - lo))
        def _(c):
            row = pl.multiple_of(8 * c, 8)
            at = pl.ds(row, 8)
            for t in range(nt):
                gg = g[t, at, :]
                xx = x[t, at, :]
                z = (sp[t, at, :] - xx) + (
                    gg * (column_conv(u, t, row) - 4.0 * xx)
                    + r[t, at, :] * column_conv(w, t, row)
                )
                d[t, at, :] = c1 * d[t, at, :] + c2 * z

    half = SWEEPS // 2

    @pl.loop(0, half)
    def _(k):
        sweep(k, 1, n_ext - 1)

    @pl.loop(half, SWEEPS - 1)
    def _(k):
        sweep(k, 2, n_ext - 2)

    near = rows + 16
    first_row = HALO - 8

    @pl.loop(0, near // 16)
    def _(c):
        row = pl.multiple_of(16 * c, 16)
        at = pl.ds(pl.multiple_of(row + first_row, 8), 16)
        for t in range(nt):
            split(x[t, at, :] + d[t, at, :], pl.ds(row, 16), t)

    moved = jnp.dot(lhs[0:near, :], to_plain[...], preferred_element_type=F32)
    for t in range(nt):
        xn[t, first_row : first_row + near, :] = moved[:, t * 128 : (t + 1) * 128]

    @pl.loop(0, n_rt)
    def _(c):
        row = pl.multiple_of(8 * c, 8)
        for t in range(lt):
            pot_h[pl.ds(row, 8), t * 128 : (t + 1) * 128] = xn[t, pl.ds(row + HALO, 8), :]

    @pl.when(has_dn)
    def _():
        i_up.wait_recv()

    @pl.when(has_up)
    def _():
        i_dn.wait_recv()

    i_lf.wait_recv()
    i_rt.wait_recv()

    def drift(c):
        row = pl.multiple_of(8 * c, 8)
        at = pl.ds(row + HALO, 8)
        left, right = shifts([xn[t, at, :] for t in range(nt)])
        de = [
            -0.5 * (xn[t, pl.ds(row + HALO + 1, 8), :] - xn[t, pl.ds(row + HALO - 1, 8), :])
            for t in range(lt)
        ]
        dn_ = [0.5 * (right[t] - left[t]) for t in range(lt)]
        return row, de, dn_

    mx[...] = jnp.zeros((8, 128), F32)

    @pl.loop(0, n_rt)
    def _(c):
        row, de, dn_ = drift(c)
        best = mx[...]
        for t in range(lt):
            best = jnp.maximum(best, jnp.abs(de[t]) + jnp.abs(dn_[t]))
        mx[...] = best

    lat_copies = []
    for o in range(1, nlat):
        lat_copies.append(
            pltpu.make_async_remote_copy(
                src_ref=mx, dst_ref=rx_lat.at[o - 1],
                send_sem=ss_lat.at[o - 1], recv_sem=rs_lat.at[o - 1],
                device_id=(lax.rem(me_lat + o, nlat), me_lon), device_id_type=MESH,
            )
        )
        lat_copies[-1].start()

    def fluxes(s, lo, hi):
        @pl.loop(lo, hi)
        def _(c):
            row, de, dn_ = drift(c)
            at = pl.ds(row + 8, 8)
            tiles = [ion[s, t, at, :] for t in range(lt)]
            tiles.append(
                jnp.where(
                    lane < 64,
                    pltpu.roll(ion_fr[pl.ds(row, 8), :], (128 - 32 * s) % 128, 1),
                    pltpu.roll(ion_fl[pl.ds(row, 8), :], 96 - 32 * s, 1),
                )
            )
            left, right = shifts(tiles)
            for t in range(lt):
                n = tiles[t]
                f = jnp.maximum(de[t], 0.0) * (n - left[t])
                f = f + jnp.minimum(de[t], 0.0) * (right[t] - n)
                f = f + jnp.maximum(dn_[t], 0.0) * (n - ion[s, t, pl.ds(row + 7, 8), :])
                f = f + jnp.minimum(dn_[t], 0.0) * (ion[s, t, pl.ds(row + 9, 8), :] - n)
                flux[s, t, pl.ds(row, 8), :] = f

    fluxes(0, 0, n_rt)
    fluxes(1, 0, n_rt)
    best = mx[...]
    for o in range(1, nlat):
        lat_copies[o - 1].wait_recv()
        best = jnp.maximum(best, rx_lat[o - 1])
    mx2[...] = best
    lon_copies = []
    for o in range(1, nlon):
        lon_copies.append(
            pltpu.make_async_remote_copy(
                src_ref=mx2, dst_ref=rx_lon.at[o - 1],
                send_sem=ss_lon.at[o - 1], recv_sem=rs_lon.at[o - 1],
                device_id=(me_lat, lax.rem(me_lon + o, nlon)), device_id_type=MESH,
            )
        )
        lon_copies[-1].start()
    fluxes(2, 0, n_rt)
    best = mx2[...]
    for o in range(1, nlon):
        lon_copies[o - 1].wait_recv()
        best = jnp.maximum(best, rx_lon[o - 1])
    best = jnp.max(best, axis=0, keepdims=True)
    best = jnp.max(best, axis=1, keepdims=True)
    step = jnp.broadcast_to(COURANT / (best + 1e-6), (8, 128))

    for s in range(3):
        scale = MOBILITY[s] * step

        @pl.loop(0, n_rt)
        def _(c):
            row = pl.multiple_of(8 * c, 8)
            for t in range(lt):
                upd_h[s, pl.ds(row, 8), t * 128 : (t + 1) * 128] = (
                    ion[s, t, pl.ds(row + 8, 8), :] - scale * flux[s, t, pl.ds(row, 8), :]
                )

    @pl.when(has_up)
    def _():
        for c in [n_up, i_up] + ups:
            c.wait_send()

    @pl.when(has_dn)
    def _():
        for c in [n_dn, i_dn] + dns:
            c.wait_send()

    for c in [i_lf, i_rt, e_lf, e_rt] + sig_copies + [c for _, c in t_copies] + lons + lat_copies + lon_copies:
        c.wait_send()


def solution(mesh):
    nlat, nlon = mesh.shape["lat"], mesh.shape["lon"]
    theta, first_list, second_list = chebyshev_factors()

    def shards(pedersen, hall_conductivity, east_wind, north_wind, ion_density):
        lev, rows, cols = pedersen.shape
        lt = cols // 128
        nt = lt + 1
        ext = rows + 2 * HALO
        vm = lambda *shape: pltpu.VMEM(shape, F32)
        half = lambda *shape: pltpu.VMEM(shape, jnp.bfloat16)
        dma = lambda *shape: pltpu.SemaphoreType.DMA(shape)
        coef = jnp.array([first_list, second_list], F32)
        anyspec = pl.BlockSpec(memory_space=pl.ANY)
        return pl.pallas_call(
            functools.partial(kernel, nlat, nlon, lev, rows, lt),
            out_shape=(
                jax.ShapeDtypeStruct((rows, cols), F32),
                jax.ShapeDtypeStruct((3, rows, cols), F32),
            ),
            in_specs=[pl.BlockSpec(memory_space=pltpu.SMEM)] + [anyspec] * 5,
            out_specs=(pl.BlockSpec(memory_space=pltpu.VMEM),) * 2,
            scratch_shapes=[vm(lev, rows, cols)] * 4
            + [vm(3, lt, rows + 16, 128), vm(rows, 128), vm(rows, 128)] + [vm(rows, 128)] * 2
            + [vm(lt, rows, 128), vm(lt, rows, 128), vm(lt, rows + 16, 128)]
            + [vm(rows, 128)] * 2
            + [vm(lt, rows, 128)] * 4
            + [vm(nt, ext, 128)] * 3
            + [half(2 * ext, 3 * nt * 128)] + [half(3 * nt * 128, nt * 128)] * 2 + [vm(nt, ext, 128)]
            + [vm(ext, 128)] * 4
            + [vm(nt, ext, 128)] * 7
            + [vm(3, lt, rows, 128)]
            + [vm(8, 128), vm(nlat - 1, 8, 128), vm(8, 128), vm(nlon - 1, 8, 128)]
            + [dma(rows // 8, 4), dma(3, lt), dma(32), dma(32)]
            + [dma(nlat - 1)] * 2
            + [dma(nlon - 1)] * 2,
            compiler_params=pltpu.CompilerParams(
                collective_id=0, has_side_effects=True, vmem_limit_bytes=60 * 1024 * 1024
            ),
        )(coef, pedersen, hall_conductivity, east_wind, north_wind, ion_density)

    spec = P(None, "lat", "lon")
    return jax.shard_map(
        shards,
        mesh=mesh,
        in_specs=(spec,) * 5,
        out_specs=(P("lat", "lon"), spec),
        check_vma=False,
    )
```

```python
import functools

import jax
import jax.numpy as jnp
from jax import lax
from jax.experimental import pallas as pl
from jax.experimental.pallas import tpu as pltpu
from jax.sharding import PartitionSpec as P

SWEEPS = 16
DAMPING = 0.0001
LOW_BOUND = 0.05
HIGH_BOUND = 2.0
COURANT = 0.8
MOBILITY = (1.0, 0.6, 0.3)
MESH = pl.DeviceIdType.MESH
HALO = 24
F32 = jnp.float32


def chebyshev_factors():
    theta = 0.5 * (HIGH_BOUND + LOW_BOUND)
    delta = 0.5 * (HIGH_BOUND - LOW_BOUND)
    sigma_one = theta / delta
    rho_prev = 1.0 / sigma_one
    first_list = []
    second_list = []
    for sweep in range(SWEEPS):
        rho_next = 1.0 / (2.0 * sigma_one - rho_prev)
        first_list.append(rho_next * rho_prev)
        second_list.append(2.0 * rho_next / delta)
        rho_prev = rho_next
    return (theta, first_list, second_list)


def unroll_of(count):
    return max(k for k in range(1, 11) if count % k == 0)


def kernel(
    nlat, nlon, lev, rows, lt,
    coef, ped_h, hall_h, east_h, north_h, ion_h,
    pot_h, upd_h,
    ped, hall, east, north,
    ion, ipk_l, ipk_r, ion_fr, ion_fl,
    sig, cur_e, cur_n, epk_l, epk_r, e_rx_r, e_rx_l, e_fr, e_fl, s_one, t_out, sig_rx, t_rx,
    S, src, SS, lhs, to_strided, to_plain, xn, pk_l, pk_r, rx_fr, rx_fl,
    g, r, sp, x, d, u, w,
    flux, mx, rx_lat, mx2, rx_lon,
    sem_in, sem_ion, ss, rs, ss_lat, rs_lat, ss_lon, rs_lon,
):
    n_rt = rows // 8
    nt = lt + 1
    me_lat = lax.axis_index("lat")
    me_lon = lax.axis_index("lon")
    has_up = me_lat > 0
    has_dn = me_lat < nlat - 1
    up = (jnp.maximum(me_lat - 1, 0), me_lon)
    dn = (jnp.minimum(me_lat + 1, nlat - 1), me_lon)
    lf = (me_lat, lax.rem(me_lon + nlon - 1, nlon))
    rt = (me_lat, lax.rem(me_lon + 1, nlon))
    mirror = (nlat - 1 - me_lat, me_lon)

    order = [0, n_rt - 1] + list(range(1, n_rt - 1))
    hbm_in = (ped_h, hall_h, east_h, north_h)
    vm_in = (ped, hall, east, north)

    def in_copy(a, row, slot):
        return pltpu.make_async_copy(
            hbm_in[a].at[:, pl.ds(row, 8), :], vm_in[a].at[:, pl.ds(row, 8), :], sem_in.at[slot, a]
        )

    def ion_copy(s, t):
        return pltpu.make_async_copy(
            ion_h.at[s, :, t * 128 : (t + 1) * 128], ion.at[s, t, 8 : 8 + rows], sem_ion.at[s, t]
        )

    for c in order[:2]:
        for a in range(4):
            in_copy(a, 8 * c, c).start()
    for s in range(3):
        for t in range(lt):
            ion_copy(s, t).start()
    for c in order[2:]:
        for a in range(4):
            in_copy(a, 8 * c, c).start()

    barrier = pltpu.get_barrier_semaphore()
    for o in range(1, nlat):
        pl.semaphore_signal(
            barrier, inc=1, device_id=(lax.rem(me_lat + o, nlat), me_lon), device_id_type=MESH
        )
    for o in range(1, nlon):
        pl.semaphore_signal(
            barrier, inc=1, device_id=(me_lat, lax.rem(me_lon + o, nlon)), device_id_type=MESH
        )
    pl.semaphore_wait(barrier, nlat + nlon - 2)

    def rcopy(src_ref, dst_ref, k, dev):
        return pltpu.make_async_remote_copy(
            src_ref=src_ref, dst_ref=dst_ref, send_sem=ss.at[k], recv_sem=rs.at[k],
            device_id=dev, device_id_type=MESH,
        )

    lane = lax.broadcasted_iota(jnp.int32, (8, 128), 1)
    sub = lax.broadcasted_iota(jnp.int32, (8, 128), 0)

    def shifts(v):
        m = len(v)
        a = [pltpu.roll(t, 1, 1) for t in v]
        b = [pltpu.roll(t, 127, 1) for t in v]
        left = [jnp.where(lane == 0, a[j - 1], a[j]) for j in range(m)]
        right = [jnp.where(lane == 127, b[(j + 1) % m], b[j]) for j in range(m)]
        return left, right

    def rev8(v):
        v = pltpu.roll(v, 4, 0)
        for b in (2, 1):
            v = jnp.where((sub & b) == 0, pltpu.roll(v, 8 - b, 0), pltpu.roll(v, b, 0))
        return v

    weight = [(0.5 + l / lev) / lev for l in range(lev)]

    def columns(c):
        row = pl.multiple_of(8 * c, 8)
        for a in range(4):
            in_copy(a, row, c).wait()
        for t in range(lt):
            at = (pl.ds(row, 8), slice(t * 128, (t + 1) * 128))
            acc = [jnp.zeros((8, 128), F32)] * 3
            for l in range(lev):
                p, h = weight[l] * ped[(l,) + at], weight[l] * hall[(l,) + at]
                e, n = east[(l,) + at], north[(l,) + at]
                acc = [acc[0] + p, acc[1] + (p * e + h * n), acc[2] + (p * n - h * e)]
            sig[t, pl.ds(row, 8), :] = acc[0]
            cur_e[t, pl.ds(row, 8), :] = acc[1]
            cur_n[t, pl.ds(row + 8, 8), :] = acc[2]

    def both(lo, hi):
        @pl.loop(lo, hi)
        def _(c):
            columns(c)

    both(0, 1)
    both(n_rt - 1, n_rt)
    n_up = rcopy(cur_n.at[:, 8:16], cur_n.at[:, rows + 8 : rows + 16], 0, up)
    n_dn = rcopy(cur_n.at[:, rows : rows + 8], cur_n.at[:, 0:8], 1, dn)
    i_up = rcopy(ion.at[:, :, 8:16], ion.at[:, :, rows + 8 : rows + 16], 2, up)
    i_dn = rcopy(ion.at[:, :, rows : rows + 8], ion.at[:, :, 0:8], 3, dn)
    i_lf = rcopy(ipk_l, ion_fr, 4, lf)
    i_rt = rcopy(ipk_r, ion_fl, 5, rt)

    for s in range(3):
        for t in range(lt):
            ion_copy(s, t).wait()

    @pl.when(has_up)
    def _():
        n_up.start()
        i_up.start()

    @pl.when(has_dn)
    def _():
        n_dn.start()
        i_dn.start()

    @pl.when(jnp.logical_not(has_up))
    def _():
        cur_n[:, 0:8, :] = jnp.zeros((lt, 8, 128), F32)
        ion[:, :, 0:8, :] = jnp.zeros((3, lt, 8, 128), F32)

    @pl.when(jnp.logical_not(has_dn))
    def _():
        cur_n[:, rows + 8 : rows + 16, :] = jnp.zeros((lt, 8, 128), F32)
        ion[:, :, rows + 8 : rows + 16, :] = jnp.zeros((3, lt, 8, 128), F32)

    pieces = 4
    per = n_rt // pieces
    sig_copies = []
    for q in range(pieces):
        both(max(1, q * per), min(n_rt - 1, (q + 1) * per))
        band = slice(q * per * 8, (q + 1) * per * 8)
        copy = rcopy(sig.at[:, band], sig_rx.at[:, band], 6 + q, mirror)
        copy.start()
        sig_copies.append(copy)

    for o in range(n_rt // 8):
        for t, skip, out in ((0, 0, epk_l), (lt - 1, 16, epk_r)):
            acc = None
            for k in range(8):
                lo = 64 * o + 8 * k
                v = cur_e[t, lo : lo + 8, :]
                turn = (16 * k + skip) % 128
                v = pltpu.roll(v, turn, 1) if turn else v
                acc = v if k == 0 else jnp.where(lane < 16 * k, acc, v)
            out[8 * o : 8 * o + 8, :] = acc

    e_lf = rcopy(epk_l, e_rx_r, 10, lf)
    e_rt = rcopy(epk_r, e_rx_l, 11, rt)
    e_lf.start()
    e_rt.start()

    @pl.loop(0, n_rt)
    def _(c):
        at = pl.ds(pl.multiple_of(8 * c, 8), 8)
        inner = pl.ds(pl.multiple_of(8 * c + 8, 8), 8)
        a, b = [], []
        for s in range(3):
            v, q = ion[s, 0, inner, :], ion[s, lt - 1, inner, :]
            a.append(pltpu.roll(v, 32 * s, 1) if s else v)
            b.append(pltpu.roll(q, 32 * (s + 1), 1))
        ipk_l[at, :] = jnp.where(lane < 32, a[0], jnp.where(lane < 64, a[1], a[2]))
        ipk_r[at, :] = jnp.where(lane < 32, b[0], jnp.where(lane < 64, b[1], b[2]))

    i_lf.start()
    i_rt.start()

    @pl.when(has_dn)
    def _():
        n_up.wait_recv()

    @pl.when(has_up)
    def _():
        n_dn.wait_recv()

    e_lf.wait_recv()
    e_rt.wait_recv()
    for o in range(n_rt // 8):
        part = slice(8 * o, 8 * o + 8)
        for k in range(8):
            lo = 64 * o + 8 * k
            v, q = e_rx_r[part, :], e_rx_l[part, :]
            e_fr[lo : lo + 8, :] = pltpu.roll(v, 128 - 16 * k, 1) if k else v
            e_fl[lo : lo + 8, :] = pltpu.roll(q, 112 - 16 * k, 1) if k < 7 else q

    t_copies = []
    for q in [0, pieces - 1] + list(range(1, pieces - 1)):
        @pl.loop(q * per, (q + 1) * per)
        def _(c):
            row = pl.multiple_of(8 * c, 8)
            tiles = [cur_e[t, pl.ds(row, 8), :] for t in range(lt)]
            tiles.append(jnp.where(lane < 64, e_fr[pl.ds(row, 8), :], e_fl[pl.ds(row, 8), :]))
            left, right = shifts(tiles)
            for t in range(lt):
                d_lon = 0.5 * (right[t] - left[t])
                d_lat = 0.5 * (cur_n[t, pl.ds(row + 9, 8), :] - cur_n[t, pl.ds(row + 7, 8), :])
                s_one[t, pl.ds(row, 8), :] = d_lon + d_lat
                t_out[t, pl.ds(row, 8), :] = d_lon - d_lat

        band = slice(q * per * 8, (q + 1) * per * 8)
        copy = rcopy(t_out.at[:, band], t_rx.at[:, band], 12 + q, mirror)
        copy.start()
        t_copies.append((q, copy))

    width = nt * 128

    @pl.loop(0, width // 16)
    def _(c):
        row = lax.broadcasted_iota(jnp.int32, (16, 128), 0) + 16 * c
        col = lax.broadcasted_iota(jnp.int32, (16, 128), 1)
        for t in range(nt):
            there = jnp.where(row == col * nt + t, 1.0, 0.0).astype(jnp.bfloat16)
            for part in range(3):
                at = pl.ds(pl.multiple_of(part * width + 16 * c, 16), 16)
                to_strided[at, t * 128 : (t + 1) * 128] = there

    for j in range(nt):
        @pl.loop(0, 8)
        def _(c):
            row = lax.broadcasted_iota(jnp.int32, (16, 128), 0) + 16 * c
            col = lax.broadcasted_iota(jnp.int32, (16, 128), 1)
            for t in range(nt):
                back = jnp.where(row * nt + j == col + t * 128, 1.0, 0.0).astype(jnp.bfloat16)
                for part in range(3):
                    at = pl.ds(pl.multiple_of(part * width + j * 128 + 16 * c, 16), 16)
                    to_plain[at, t * 128 : (t + 1) * 128] = back

    def split(v, at, t):
        for part in range(3):
            low = v.astype(jnp.bfloat16)
            lhs[at, part * width + t * 128 : part * width + (t + 1) * 128] = low
            v = v - low.astype(F32)

    def zero_rows(ref, lo, hi):
        ref[0:lt, lo:hi, :] = jnp.zeros((lt, hi - lo, 128), F32)

    @pl.when(jnp.logical_not(has_up))
    def _():
        zero_rows(S, 0, HALO)
        zero_rows(src, 0, HALO)

    @pl.when(jnp.logical_not(has_dn))
    def _():
        zero_rows(S, HALO + rows, 2 * HALO + rows)
        zero_rows(src, HALO + rows, 2 * HALO + rows)

    def combine(own, rx, out, q):
        @pl.loop((pieces - 1 - q) * per, (pieces - q) * per)
        def _(c):
            row = pl.multiple_of(8 * c, 8)
            back = pl.multiple_of(rows - 8 - 8 * c, 8)
            for t in range(lt):
                out[t, pl.ds(row + HALO, 8), :] = own[t, pl.ds(row, 8), :] + rev8(
                    rx[t, pl.ds(back, 8), :]
                )

    for q in range(pieces):
        sig_copies[q].wait_recv()
        combine(sig, sig_rx, S, q)
    lo_in, lo_out = slice(HALO, 2 * HALO), slice(0, HALO)
    hi_in, hi_out = slice(rows, rows + HALO), slice(rows + HALO, rows + 2 * HALO)
    ups = [
        rcopy(f.at[0:lt, lo_in], f.at[0:lt, hi_out], 16 + k, up) for k, f in enumerate((S, src))
    ]
    dns = [
        rcopy(f.at[0:lt, hi_in], f.at[0:lt, lo_out], 18 + k, dn) for k, f in enumerate((S, src))
    ]

    def pack(lo, hi):
        @pl.loop(lo // 8, hi // 8)
        def _(c):
            at = pl.ds(pl.multiple_of(8 * c, 8), 8)
            pk_l[at, :] = jnp.where(lane < 64, S[0, at, :], pltpu.roll(src[0, at, :], 64, 1))
            pk_r[at, :] = jnp.where(
                lane >= 64, S[lt - 1, at, :], pltpu.roll(src[lt - 1, at, :], 64, 1)
            )

    lons = []

    def send_lon(part, k):
        lons.append(rcopy(pk_l.at[part], rx_fr.at[part], k, lf))
        lons.append(rcopy(pk_r.at[part], rx_fl.at[part], k + 1, rt))
        lons[-2].start()
        lons[-1].start()

    for i, (q, copy) in enumerate(t_copies):
        copy.wait_recv()
        combine(s_one, t_rx, src, q)
        if i == 1:
            @pl.when(has_up)
            def _():
                for c in ups:
                    c.start()

            @pl.when(has_dn)
            def _():
                for c in dns:
                    c.start()

        lo = HALO + (pieces - 1 - q) * per * 8
        pack(lo, lo + per * 8)
        send_lon(slice(lo, lo + per * 8), 20 + 2 * i)

    @pl.when(has_up)
    def _():
        for c in dns:
            c.wait_recv()

    pack(0, HALO)
    send_lon(lo_out, 28)

    @pl.when(has_dn)
    def _():
        for c in ups:
            c.wait_recv()

    pack(HALO + rows, 2 * HALO + rows)
    send_lon(hi_out, 30)
    for c in lons:
        c.wait_recv()

    n_ext = (rows + 2 * HALO) // 8
    total = rows * nlat

    lane16 = lax.broadcasted_iota(jnp.int32, (16, 128), 1)
    ext = 8 * n_ext

    @pl.loop(0, n_ext // 2)
    def _(c):
        row = pl.multiple_of(16 * c, 16)
        at = pl.ds(row, 16)
        at2 = pl.ds(pl.multiple_of(row + ext, 16), 16)
        fr, fl = rx_fr[at, :], rx_fl[at, :]
        for t in range(lt):
            split(S[t, at, :], at, t)
            split(src[t, at, :], at2, t)
        split(jnp.where(lane16 < 64, fr, fl), at, lt)
        split(pltpu.roll(jnp.where(lane16 >= 64, fr, fl), 64, 1), at2, lt)

    for f, out in enumerate((SS, sp)):
        moved = jnp.dot(
            lhs[f * ext : (f + 1) * ext, :], to_strided[...], preferred_element_type=F32
        )
        for t in range(nt):
            out[t, :, :] = moved[:, t * 128 : (t + 1) * 128]

    def smooth_strided(v):
        left = [pltpu.roll(v[-1], 1, 1)] + v[:-1]
        right = v[1:] + [pltpu.roll(v[0], 127, 1)]
        return [t + 0.5 * (p + q) for t, p, q in zip(v, left, right)]

    @pl.loop(0, n_ext)
    def _(c):
        at = pl.ds(pl.multiple_of(8 * c, 8), 8)
        for t, v in enumerate(smooth_strided([SS[t, at, :] for t in range(nt)])):
            u[t, at, :] = v
            w[t, at, :] = jnp.zeros((8, 128), F32)

    theta = 0.5 * (HIGH_BOUND + LOW_BOUND)

    def column_conv(ref, t, row):
        return (
            ref[t, pl.ds(row - 1, 8), :] + ref[t, pl.ds(row + 1, 8), :]
        ) + 2.0 * ref[t, pl.ds(row, 8), :]

    @pl.loop(1, n_ext - 1)
    def _(c):
        row = pl.multiple_of(8 * c, 8)
        at = pl.ds(row, 8)
        where = sub + (row - HALO + me_lat * rows)
        inside = (where >= 0) & (where < total)
        for t in range(nt):
            s = SS[t, at, :]
            diag = DAMPING + 0.5 * (4.0 * s + column_conv(u, t, row))
            inv = jnp.where(inside, 1.0 / diag, 0.0)
            half = 0.5 * inv
            r[t, at, :] = half
            g[t, at, :] = half * s
            first = sp[t, at, :] * inv
            sp[t, at, :] = first
            d[t, at, :] = first * (1.0 / theta)
            x[t, at, :] = jnp.zeros((8, 128), F32)

    def sweep(k, lo, hi):
        c1 = coef[0, k]
        c2 = coef[1, k]

        @pl.loop(lo, hi, unroll=unroll_of(hi - lo))
        def _(c):
            at = pl.ds(pl.multiple_of(8 * c, 8), 8)
            xs = [x[t, at, :] + d[t, at, :] for t in range(nt)]
            ys = [SS[t, at, :] * xs[t] for t in range(nt)]
            us = smooth_strided(xs)
            ws = smooth_strided(ys)
            for t in range(nt):
                x[t, at, :] = xs[t]
                u[t, at, :] = us[t]
                w[t, at, :] = ws[t]

        @pl.loop(lo, hi, unroll=unroll_of(hi - lo))
        def _(c):
            row = pl.multiple_of(8 * c, 8)
            at = pl.ds(row, 8)
            for t in range(nt):
                gg = g[t, at, :]
                xx = x[t, at, :]
                z = (sp[t, at, :] - xx) + (
                    gg * (column_conv(u, t, row) - 4.0 * xx)
                    + r[t, at, :] * column_conv(w, t, row)
                )
                d[t, at, :] = c1 * d[t, at, :] + c2 * z

    half = SWEEPS // 2

    @pl.loop(0, half)
    def _(k):
        sweep(k, 1, n_ext - 1)

    @pl.loop(half, SWEEPS - 1)
    def _(k):
        sweep(k, 2, n_ext - 2)

    near = rows + 16
    first_row = HALO - 8

    @pl.loop(0, near // 16)
    def _(c):
        row = pl.multiple_of(16 * c, 16)
        at = pl.ds(pl.multiple_of(row + first_row, 8), 16)
        for t in range(nt):
            split(x[t, at, :] + d[t, at, :], pl.ds(row, 16), t)

    moved = jnp.dot(lhs[0:near, :], to_plain[...], preferred_element_type=F32)
    for t in range(nt):
        xn[t, first_row : first_row + near, :] = moved[:, t * 128 : (t + 1) * 128]

    @pl.loop(0, n_rt)
    def _(c):
        row = pl.multiple_of(8 * c, 8)
        for t in range(lt):
            pot_h[pl.ds(row, 8), t * 128 : (t + 1) * 128] = xn[t, pl.ds(row + HALO, 8), :]

    @pl.when(has_dn)
    def _():
        i_up.wait_recv()

    @pl.when(has_up)
    def _():
        i_dn.wait_recv()

    i_lf.wait_recv()
    i_rt.wait_recv()

    def drift(c):
        row = pl.multiple_of(8 * c, 8)
        at = pl.ds(row + HALO, 8)
        left, right = shifts([xn[t, at, :] for t in range(nt)])
        de = [
            -0.5 * (xn[t, pl.ds(row + HALO + 1, 8), :] - xn[t, pl.ds(row + HALO - 1, 8), :])
            for t in range(lt)
        ]
        dn_ = [0.5 * (right[t] - left[t]) for t in range(lt)]
        return row, de, dn_

    mx[...] = jnp.zeros((8, 128), F32)

    @pl.loop(0, n_rt)
    def _(c):
        row, de, dn_ = drift(c)
        best = mx[...]
        for t in range(lt):
            best = jnp.maximum(best, jnp.abs(de[t]) + jnp.abs(dn_[t]))
        mx[...] = best

    lat_copies = []
    for o in range(1, nlat):
        lat_copies.append(
            pltpu.make_async_remote_copy(
                src_ref=mx, dst_ref=rx_lat.at[o - 1],
                send_sem=ss_lat.at[o - 1], recv_sem=rs_lat.at[o - 1],
                device_id=(lax.rem(me_lat + o, nlat), me_lon), device_id_type=MESH,
            )
        )
        lat_copies[-1].start()

    def fluxes(s, lo, hi):
        @pl.loop(lo, hi)
        def _(c):
            row, de, dn_ = drift(c)
            at = pl.ds(row + 8, 8)
            tiles = [ion[s, t, at, :] for t in range(lt)]
            tiles.append(
                jnp.where(
                    lane < 64,
                    pltpu.roll(ion_fr[pl.ds(row, 8), :], (128 - 32 * s) % 128, 1),
                    pltpu.roll(ion_fl[pl.ds(row, 8), :], 96 - 32 * s, 1),
                )
            )
            left, right = shifts(tiles)
            for t in range(lt):
                n = tiles[t]
                f = jnp.maximum(de[t], 0.0) * (n - left[t])
                f = f + jnp.minimum(de[t], 0.0) * (right[t] - n)
                f = f + jnp.maximum(dn_[t], 0.0) * (n - ion[s, t, pl.ds(row + 7, 8), :])
                f = f + jnp.minimum(dn_[t], 0.0) * (ion[s, t, pl.ds(row + 9, 8), :] - n)
                flux[s, t, pl.ds(row, 8), :] = f

    fluxes(0, 0, n_rt)
    fluxes(1, 0, n_rt)
    best = mx[...]
    for o in range(1, nlat):
        lat_copies[o - 1].wait_recv()
        best = jnp.maximum(best, rx_lat[o - 1])
    mx2[...] = best
    lon_copies = []
    for o in range(1, nlon):
        lon_copies.append(
            pltpu.make_async_remote_copy(
                src_ref=mx2, dst_ref=rx_lon.at[o - 1],
                send_sem=ss_lon.at[o - 1], recv_sem=rs_lon.at[o - 1],
                device_id=(me_lat, lax.rem(me_lon + o, nlon)), device_id_type=MESH,
            )
        )
        lon_copies[-1].start()
    fluxes(2, 0, n_rt)
    best = mx2[...]
    for o in range(1, nlon):
        lon_copies[o - 1].wait_recv()
        best = jnp.maximum(best, rx_lon[o - 1])
    best = jnp.max(best, axis=0, keepdims=True)
    best = jnp.max(best, axis=1, keepdims=True)
    step = jnp.broadcast_to(COURANT / (best + 1e-6), (8, 128))

    for s in range(3):
        scale = MOBILITY[s] * step

        @pl.loop(0, n_rt)
        def _(c):
            row = pl.multiple_of(8 * c, 8)
            for t in range(lt):
                upd_h[s, pl.ds(row, 8), t * 128 : (t + 1) * 128] = (
                    ion[s, t, pl.ds(row + 8, 8), :] - scale * flux[s, t, pl.ds(row, 8), :]
                )

    @pl.when(has_up)
    def _():
        for c in [n_up, i_up] + ups:
            c.wait_send()

    @pl.when(has_dn)
    def _():
        for c in [n_dn, i_dn] + dns:
            c.wait_send()

    for c in [i_lf, i_rt, e_lf, e_rt] + sig_copies + [c for _, c in t_copies] + lons + lat_copies + lon_copies:
        c.wait_send()


def write_out(pot_v, upd_v, pot_h, upd_h, sem):
    copies = [
        pltpu.make_async_copy(upd_v, upd_h, sem.at[1]),
        pltpu.make_async_copy(pot_v, pot_h, sem.at[0]),
    ]
    for c in copies:
        c.start()
    for c in copies:
        c.wait()


def solution(mesh):
    nlat, nlon = mesh.shape["lat"], mesh.shape["lon"]
    theta, first_list, second_list = chebyshev_factors()

    def shards(pedersen, hall_conductivity, east_wind, north_wind, ion_density):
        lev, rows, cols = pedersen.shape
        lt = cols // 128
        nt = lt + 1
        ext = rows + 2 * HALO
        vm = lambda *shape: pltpu.VMEM(shape, F32)
        half = lambda *shape: pltpu.VMEM(shape, jnp.bfloat16)
        dma = lambda *shape: pltpu.SemaphoreType.DMA(shape)
        coef = jnp.array([first_list, second_list], F32)
        anyspec = pl.BlockSpec(memory_space=pl.ANY)
        pot, upd = pl.pallas_call(
            functools.partial(kernel, nlat, nlon, lev, rows, lt),
            out_shape=(
                jax.ShapeDtypeStruct((rows, cols), F32),
                jax.ShapeDtypeStruct((3, rows, cols), F32),
            ),
            in_specs=[pl.BlockSpec(memory_space=pltpu.SMEM)] + [anyspec] * 5,
            out_specs=(pl.BlockSpec(memory_space=pltpu.VMEM),) * 2,
            scratch_shapes=[vm(lev, rows, cols)] * 4
            + [vm(3, lt, rows + 16, 128), vm(rows, 128), vm(rows, 128)] + [vm(rows, 128)] * 2
            + [vm(lt, rows, 128), vm(lt, rows, 128), vm(lt, rows + 16, 128)]
            + [vm(rows // 8, 128)] * 4
            + [vm(rows, 128)] * 2
            + [vm(lt, rows, 128)] * 4
            + [vm(nt, ext, 128)] * 3
            + [half(2 * ext, 3 * nt * 128)] + [half(3 * nt * 128, nt * 128)] * 2 + [vm(nt, ext, 128)]
            + [vm(ext, 128)] * 4
            + [vm(nt, ext, 128)] * 7
            + [vm(3, lt, rows, 128)]
            + [vm(8, 128), vm(nlat - 1, 8, 128), vm(8, 128), vm(nlon - 1, 8, 128)]
            + [dma(rows // 8, 4), dma(3, lt), dma(32), dma(32)]
            + [dma(nlat - 1)] * 2
            + [dma(nlon - 1)] * 2,
            compiler_params=pltpu.CompilerParams(
                collective_id=0, has_side_effects=True, vmem_limit_bytes=60 * 1024 * 1024
            ),
        )(coef, pedersen, hall_conductivity, east_wind, north_wind, ion_density)
        return pl.pallas_call(
            write_out,
            out_shape=(
                jax.ShapeDtypeStruct((rows, cols), F32),
                jax.ShapeDtypeStruct((3, rows, cols), F32),
            ),
            in_specs=[pl.BlockSpec(memory_space=pltpu.VMEM)] * 2,
            out_specs=(anyspec, anyspec),
            scratch_shapes=[dma(2)],
        )(pot, upd)

    spec = P(None, "lat", "lon")
    return jax.shard_map(
        shards,
        mesh=mesh,
        in_specs=(spec,) * 5,
        out_specs=(P("lat", "lon"), spec),
        check_vma=False,
    )
```
